512 devices in a mesh: head: 32 (over x, y), kv: 16 (over z, core).
Axes of the slice: x: 4, y: 8, z: 8, core: 2. Of those that a mesh axis runs over, the one named last changes fastest.
Arguments:
- queries: bfloat16 [2048, 4096], P(('head', 'kv')), may hold values from -240 to 240
- new_keys: bfloat16 [2048, 1024], P(('head', 'kv')), may hold values from -6 to 6
- new_values: bfloat16 [2048, 1024], P(('head', 'kv')), may hold values from -6 to 6
- cache_keys: bfloat16 [8, 16384, 128], P(None, 'kv'), may hold values from -6 to 6
- cache_values: bfloat16 [8, 16384, 128], P(None, 'kv'), may hold values from -6 to 6
- start: int32 [1], replicated, may hold values from 16384 to 28672
Outputs:
- attended: bfloat16 [2048, 4096], P(('head', 'kv'))
The draws below stay inside these ranges and needn't reach their ends.
All inputs are finite; a program needn't handle non-finite values.
Results may differ from the reference program's by a relative error of at most 0.034.
Values may be sent and summed in bfloat16 or wider, within the bound.
A program may use at most 128 MiB of HBM per device.

```python
import jax
import jax.numpy as jnp
from jax import lax

HEADS = 32
KVH = 8
HD = 128
STRETCH = 2048
CACHE = 16384


def draw_queries(key, part):
    values = jnp.clip(jax.random.normal(key, (STRETCH, HEADS * HD), jnp.float32), -4.0, 4.0)
    return values.astype(jnp.bfloat16)


def block_scale(own_key, shape, pieces, least, top_value):
    def one(dim, parts):
        draws = jax.random.uniform(jax.random.fold_in(jax.random.fold_in(own_key, 6), dim), (parts,), jnp.float32, least / len(pieces), top_value / len(pieces))
        return jnp.repeat(jnp.exp(draws), shape[dim] // parts).reshape((-1,) + (1,) * (len(shape) - dim - 1))

    level = one(*pieces[0])
    for cut in pieces[1:]:
        level = level * one(*cut)
    return level


def scatter_about(own_key, extent, scale, most, cuts=(), held_as=jnp.bfloat16):
    entries = jax.random.normal(own_key, extent, jnp.float32) * scale
    if len(cuts) > 0:
        entries = block_scale(own_key, extent, cuts, -0.22, 0.18) * entries
    return jnp.clip(entries, min=-most, max=most).astype(held_as)


def setup_inputs(seed: int = 0) -> dict:
    arg_keys = jax.random.split(jax.random.key(seed), 7)
    queries = draw_queries(jax.random.fold_in(arg_keys[6], 71), 0)
    new_keys = scatter_about(arg_keys[1], (STRETCH, KVH * HD), 1.0, 6.0, ((0, 512),))
    new_values = scatter_about(arg_keys[2], (STRETCH, KVH * HD), 1.0, 6.0, ((0, 512),))
    cache_keys = scatter_about(arg_keys[3], (KVH, CACHE, HD), 1.0, 6.0, ((1, 16),))
    cache_values = scatter_about(arg_keys[4], (KVH, CACHE, HD), 1.0, 6.0, ((1, 16),))
    start = jax.random.randint(arg_keys[5], (1,), CACHE, 28673).astype(jnp.int32)
    return {"queries": queries, "new_keys": new_keys, "new_values": new_values, "cache_keys": cache_keys, "cache_values": cache_values, "start": start}


THETA = 500000.0


def frequencies(width):
    half = width // 2
    base = jnp.power(THETA, -(jnp.arange(half, dtype=jnp.float32) * 2.0 / width))
    wave = 2.0 * jnp.pi / base
    smooth = (8192.0 / wave - 1.0) / 3.0
    blended = (1.0 - smooth) * base / 8.0 + smooth * base
    return jnp.where(wave < 2048.0, base, jnp.where(wave > 8192.0, base / 8.0, blended))


def rotate(field, places):
    half = field.shape[-1] // 2
    freq = frequencies(field.shape[-1])
    angle = places.astype(jnp.float32)[:, None] * freq[None, :]
    cosine = jnp.cos(angle)[:, None, :]
    sine = jnp.sin(angle)[:, None, :]
    values = field.astype(jnp.float32)
    first = values[..., :half]
    second = values[..., half:]
    return jnp.concatenate([first * cosine - second * sine, second * cosine + first * sine], -1).astype(jnp.bfloat16)


def reference(queries, new_keys, new_values, cache_keys, cache_values, start):
    places = start[0] + jnp.arange(STRETCH, dtype=jnp.int32)
    rot_queries = rotate(queries.reshape(STRETCH, HEADS, HD), places)
    rot_keys = rotate(new_keys.reshape(STRETCH, KVH, HD), places)
    values_new = new_values.reshape(STRETCH, KVH, HD)
    group = HEADS // KVH
    scale = HD ** -0.5
    block = min(512, STRETCH)
    nblocks = STRETCH // block

    def one_head(head):
        kvhead = head // group
        query_head = lax.dynamic_index_in_dim(rot_queries, head, 1, keepdims=False)
        cached_k = lax.dynamic_index_in_dim(cache_keys, kvhead, 0, keepdims=False)
        cached_v = lax.dynamic_index_in_dim(cache_values, kvhead, 0, keepdims=False)
        fresh_k = lax.dynamic_index_in_dim(rot_keys, kvhead, 1, keepdims=False)
        fresh_v = lax.dynamic_index_in_dim(values_new, kvhead, 1, keepdims=False)

        def one_block(index):
            first = (index * block).astype(jnp.int32)
            query_rows = lax.dynamic_slice_in_dim(query_head, first, block, 0)
            scores_old = jnp.dot(query_rows, cached_k.T, preferred_element_type=jnp.float32) * scale
            scores_new = jnp.dot(query_rows, fresh_k.T, preferred_element_type=jnp.float32) * scale
            targets = first + jnp.arange(block, dtype=jnp.int32)
            visible = jnp.arange(STRETCH, dtype=jnp.int32)[None, :] <= targets[:, None]
            scores_new = jnp.where(visible, scores_new, -1e30)
            top = jnp.maximum(jnp.max(scores_old, 1), jnp.max(scores_new, 1))
            probs_old = jnp.exp(scores_old - top[:, None]).astype(jnp.bfloat16)
            probs_new = jnp.where(visible, jnp.exp(scores_new - top[:, None]), 0.0).astype(jnp.bfloat16)
            total = jnp.sum(probs_old.astype(jnp.float32), 1) + jnp.sum(probs_new.astype(jnp.float32), 1)
            output = jnp.dot(probs_old, cached_v, preferred_element_type=jnp.float32)
            output = output + jnp.dot(probs_new, fresh_v, preferred_element_type=jnp.float32)
            return (output / total[:, None]).astype(jnp.bfloat16)

        return lax.map(one_block, jnp.arange(nblocks, dtype=jnp.int32)).reshape(STRETCH, HD)

    result = lax.map(one_head, jnp.arange(HEADS, dtype=jnp.int32))
    return jnp.transpose(result, (1, 0, 2)).reshape(STRETCH, HEADS * HD)
```

```python
import functools
import math

import jax
import jax.numpy as jnp
import numpy as np
from jax import lax
from jax.experimental import pallas as pl
from jax.experimental.pallas import tpu as pltpu
from jax.sharding import PartitionSpec as P

HEADS = 32
KVH = 8
HD = 128
GROUP = HEADS // KVH
THETA = 500000.0
MESH = pl.DeviceIdType.MESH

NX, NY, NZ, NC = 4, 8, 8, 2
NG = NX * NC
TOK = 4
ROWS = TOK * GROUP
CHUNK = NG * ROWS
EXP_SCALE = HD ** (-0.5) * math.log2(math.e)


def frequencies():
    half = HD // 2
    base = THETA ** (-(np.arange(half, dtype=np.float64) * 2.0 / HD))
    wave = 2.0 * np.pi / base
    smooth = (8192.0 / wave - 1.0) / 3.0
    blended = (1.0 - smooth) * base / 8.0 + smooth * base
    freq = np.where(wave < 2048.0, base, np.where(wave > 8192.0, base / 8.0, blended))
    return np.concatenate([freq, freq]).astype(np.float32)[None, :]


def kernel(
    start_ref, freq_ref, q_ref, k_ref, v_ref, ck_ref, cv_ref, o_ref,
    sq, skv, qall, kvall, kbuf, vbuf, so, ss, ro, rs, sf, of,
    csem, xsend, xrecv, qsend, qrecv, fsend, frecv, osend, orecv, ssend, srecv, rsend, rrecv,
):
    cached = ck_ref.shape[1]
    head, kv = lax.axis_index("head"), lax.axis_index("kv")
    x, y = lax.div(head, NY), lax.rem(head, NY)
    z, c = lax.div(kv, NC), lax.rem(kv, NC)
    g = x * NC + c

    def of_group(other):
        return (lax.div(other, NC) * NY + y, z * NC + lax.rem(other, NC))

    def of_plane(other):
        return (head, other * NC + c)

    def of_row(other):
        return (x * NY + other, kv)

    groups = [lax.rem(g + i, NG) for i in range(1, NG)]
    planes = [lax.rem(z + i, NZ) for i in (1, 7, 2, 6, 3, 5, 4)]
    rows = [lax.rem(y + i, NY) for i in (1, 7, 2, 6, 3, 5, 4)]

    own_k = pltpu.make_async_copy(ck_ref.at[g], kbuf.at[pl.ds(0, cached)], csem.at[0])
    own_v = pltpu.make_async_copy(cv_ref.at[g], vbuf.at[pl.ds(0, cached)], csem.at[1])
    own_k.start()
    own_v.start()

    barrier = pltpu.get_barrier_semaphore()
    peers = [of_group(i) for i in groups] + [of_plane(i) for i in planes] + [of_row(i) for i in rows]
    for peer in peers:
        pl.semaphore_signal(barrier, inc=1, device_id=peer, device_id_type=MESH)

    first = start_ref[0] + (head * (NZ * NC) + kv) * TOK
    places = first + lax.broadcasted_iota(jnp.int32, (TOK, HD), 0)
    angle = places.astype(jnp.float32) * freq_ref[...]
    lane = lax.broadcasted_iota(jnp.int32, (TOK, HD), 1)
    cosine = jnp.cos(angle)
    sine = jnp.sin(angle)
    sine = jnp.where(lane < HD // 2, -sine, sine)
    cos_q = jnp.concatenate([cosine] * GROUP, 0)
    sin_q = jnp.concatenate([sine] * GROUP, 0)
    for i in range(NG):
        part = jnp.concatenate(
            [
                q_ref[:, (i * GROUP + j) * HD : (i * GROUP + j + 1) * HD].astype(jnp.float32)
                for j in range(GROUP)
            ],
            0,
        )
        turned = part * cos_q + pltpu.roll(part, HD // 2, 1) * sin_q
        sq[i] = turned.astype(jnp.bfloat16)
        part = k_ref[:, i * HD : (i + 1) * HD].astype(jnp.float32)
        turned = part * cosine + pltpu.roll(part, HD // 2, 1) * sine
        value = v_ref[:, i * HD : (i + 1) * HD].astype(jnp.float32)
        skv[i] = jnp.concatenate([turned, value], 0).astype(jnp.bfloat16)

    pl.semaphore_wait(barrier, len(peers))

    sends = []
    partner = x * NC + (1 - c)
    for i in groups:
        copy = pltpu.make_async_remote_copy(
            src_ref=sq.at[i], dst_ref=qall.at[z, g], send_sem=xsend.at[0, i],
            recv_sem=xrecv.at[0, g], device_id=of_group(i), device_id_type=MESH,
        )
        copy.start()
        sends.append(copy)
        copy = pltpu.make_async_remote_copy(
            src_ref=skv.at[i], dst_ref=kvall.at[y, g], send_sem=xsend.at[1, i],
            recv_sem=xrecv.at[1, g], device_id=of_group(i), device_id_type=MESH,
        )
        copy.start()
        sends.append(copy)
    for i, (source, target) in enumerate(((ck_ref, kbuf), (cv_ref, vbuf))):
        copy = pltpu.make_async_remote_copy(
            src_ref=source.at[partner], dst_ref=target.at[pl.ds(cached, cached)],
            send_sem=csem.at[2 + i], recv_sem=csem.at[4 + i],
            device_id=of_group(partner), device_id_type=MESH,
        )
        copy.start()
        sends.append(copy)
    qall[z, g] = sq[g]
    kvall[y, g] = skv[g]

    for i in groups:
        pltpu.make_async_copy(qall.at[z, i], qall.at[z, i], xrecv.at[0, i]).wait()
    for i in planes:
        copy = pltpu.make_async_remote_copy(
            src_ref=qall.at[z], dst_ref=qall.at[z], send_sem=qsend.at[i],
            recv_sem=qrecv.at[z], device_id=of_plane(i), device_id_type=MESH,
        )
        copy.start()
        sends.append(copy)
    for i in groups:
        pltpu.make_async_copy(kvall.at[y, i], kvall.at[y, i], xrecv.at[1, i]).wait()
    for i in rows:
        copy = pltpu.make_async_remote_copy(
            src_ref=kvall.at[y], dst_ref=kvall.at[y], send_sem=fsend.at[i],
            recv_sem=frecv.at[y], device_id=of_row(i), device_id_type=MESH,
        )
        copy.start()
        sends.append(copy)

    own_k.wait()
    own_v.wait()
    for i, target in enumerate((kbuf, vbuf)):
        half = target.at[pl.ds(cached, cached)]
        pltpu.make_async_copy(half, half, csem.at[4 + i]).wait()
    for i in rows:
        pltpu.make_async_copy(kvall.at[i], kvall.at[i], frecv.at[i]).wait()

    for i in range(NY):
        for j in range(NG // 4):
            four = [kvall[i, j * 4 + n].astype(jnp.float32) for n in range(4)]
            place = 2 * cached + (i * NG + j * 4) * TOK
            kbuf[place : place + 16] = jnp.concatenate(
                [one[:TOK] for one in four], 0
            ).astype(jnp.bfloat16)
            vbuf[place : place + 16] = jnp.concatenate(
                [one[TOK:] for one in four], 0
            ).astype(jnp.bfloat16)

    fresh = NY * NG * TOK
    wide = 2 * CHUNK
    row = lax.broadcasted_iota(jnp.int32, (wide, fresh), 0)
    column = lax.broadcasted_iota(jnp.int32, (wide, fresh), 1)
    row_group = lax.rem(lax.div(row, ROWS), NG)
    row_token = (lax.div(row_group, NC) * NY + y) * (NZ * NC * TOK) + (
        lax.rem(row_group, NC) * TOK + lax.rem(row, TOK)
    )
    column_group = lax.rem(lax.div(column, TOK), NG)
    column_token = (
        lax.div(column_group, NC) * NY + lax.div(column, NG * TOK)
    ) * (NZ * NC * TOK) + (lax.rem(column_group, NC) * TOK + lax.rem(column, TOK))
    behind = row_token - column_token - z * (NC * TOK)
    square = (CHUNK, CHUNK)
    diagonal = lax.broadcasted_iota(jnp.int32, square, 0) == lax.broadcasted_iota(
        jnp.int32, square, 1
    )
    ones = jnp.ones((2 * cached + fresh, HD), jnp.bfloat16)

    def chunk(i, carry):
        pair = (lax.rem(z - i + NZ, NZ), lax.rem(z + i + 1, NZ))

        @pl.when(i > 0)
        def _():
            pltpu.make_async_copy(qall.at[pair[0]], qall.at[pair[0]], qrecv.at[pair[0]]).wait()

        pltpu.make_async_copy(qall.at[pair[1]], qall.at[pair[1]], qrecv.at[pair[1]]).wait()
        queries = jnp.concatenate([qall[one].reshape(CHUNK, HD) for one in pair], 0)
        scores = lax.dot_general(
            queries, kbuf[...], (((1,), (1,)), ((), ())), preferred_element_type=jnp.float32
        )
        plane = jnp.where(row < CHUNK, pair[0], pair[1]) * (NC * TOK)
        old, new = scores[:, : 2 * cached], scores[:, 2 * cached :]
        new = jnp.where(behind + plane >= 0, new, -1e30)
        top = jnp.maximum(jnp.max(old, 1, keepdims=True), jnp.max(new, 1, keepdims=True))
        top = top * EXP_SCALE
        scores = jnp.concatenate([old, new], 1)
        probs = jnp.exp2(scores * EXP_SCALE - top).astype(jnp.bfloat16)
        both = jnp.dot(
            probs, jnp.concatenate([vbuf[...], ones], 1), preferred_element_type=jnp.float32
        )
        total = both[:, HD:]
        level = top + jnp.log2(total)
        output = (both[:, :HD] / total).astype(jnp.bfloat16)
        for n in range(2):
            part = slice(n * CHUNK, (n + 1) * CHUNK)
            flat = jnp.sum(jnp.where(diagonal, level[part], 0.0), 0, keepdims=True)
            so[pair[n]] = output[part]
            ss[pair[n]] = flat

        def give(other):
            for source, target, sent, got in ((so, ro, osend, orecv), (ss, rs, ssend, srecv)):
                pltpu.make_async_remote_copy(
                    src_ref=source.at[other], dst_ref=target.at[z], send_sem=sent.at[other],
                    recv_sem=got.at[z], device_id=of_plane(other), device_id_type=MESH,
                ).start()

        @pl.when(i > 0)
        def _():
            give(pair[0])

        give(pair[1])
        return carry

    lax.fori_loop(0, NZ // 2, chunk, 0)
    ro[z] = so[z]
    rs[z] = ss[z]

    for i in planes:
        pltpu.make_async_copy(rs.at[i], rs.at[i], srecv.at[i]).wait()
        pltpu.make_async_copy(ro.at[i], ro.at[i], orecv.at[i]).wait()
    levels = rs[:, 0, :]
    weight = jnp.exp2(levels - jnp.max(levels, 0, keepdims=True))
    weight = weight / jnp.sum(weight, 0, keepdims=True)
    weight = jnp.transpose(weight)
    total = weight[:, 0:1] * ro[0].astype(jnp.float32)
    for i in range(1, NZ):
        total = total + weight[:, i : i + 1] * ro[i].astype(jnp.float32)
    sf[...] = total.astype(jnp.bfloat16).reshape(NG, ROWS, HD)
    for i in groups:
        copy = pltpu.make_async_remote_copy(
            src_ref=sf.at[i], dst_ref=of.at[g], send_sem=rsend.at[i],
            recv_sem=rrecv.at[g], device_id=of_group(i), device_id_type=MESH,
        )
        copy.start()
        sends.append(copy)
    of[g] = sf[g]
    for i in groups:
        pltpu.make_async_copy(of.at[i], of.at[i], rrecv.at[i]).wait()
    for i in range(NG):
        part = of[i].astype(jnp.float32)
        for j in range(GROUP):
            o_ref[:, (i * GROUP + j) * HD : (i * GROUP + j + 1) * HD] = part[
                j * TOK : (j + 1) * TOK
            ].astype(jnp.bfloat16)

    for copy in sends:
        copy.wait_send()
    for i in planes:
        for source, sent in ((so, osend), (ss, ssend)):
            pltpu.make_async_copy(source.at[i], source.at[i], sent.at[i]).wait()


def shards(queries, new_keys, new_values, cache_keys, cache_values, start):
    cached = cache_keys.shape[1]
    keys = 2 * cached + NY * NG * TOK
    vmem = pl.BlockSpec(memory_space=pltpu.VMEM)
    hbm = pl.BlockSpec(memory_space=pl.ANY)
    dma = pltpu.SemaphoreType.DMA
    bf16 = jnp.bfloat16
    return pl.pallas_call(
        kernel,
        out_shape=jax.ShapeDtypeStruct((TOK, HEADS * HD), bf16),
        in_specs=[pl.BlockSpec(memory_space=pltpu.SMEM), vmem, vmem, vmem, vmem, hbm, hbm],
        out_specs=vmem,
        scratch_shapes=[
            pltpu.VMEM((NG, ROWS, HD), bf16),
            pltpu.VMEM((NG, 2 * TOK, HD), bf16),
            pltpu.VMEM((NZ, NG, ROWS, HD), bf16),
            pltpu.VMEM((NY, NG, 2 * TOK, HD), bf16),
            pltpu.VMEM((keys, HD), bf16),
            pltpu.VMEM((keys, HD), bf16),
            pltpu.VMEM((NZ, CHUNK, HD), bf16),
            pltpu.VMEM((NZ, 1, CHUNK), jnp.float32),
            pltpu.VMEM((NZ, CHUNK, HD), bf16),
            pltpu.VMEM((NZ, 1, CHUNK), jnp.float32),
            pltpu.VMEM((NG, ROWS, HD), bf16),
            pltpu.VMEM((NG, ROWS, HD), bf16),
            dma((6,)), dma((2, NG)), dma((2, NG)), dma((NZ,)), dma((NZ,)), dma((NY,)), dma((NY,)),
            dma((NZ,)), dma((NZ,)), dma((NZ,)), dma((NZ,)), dma((NG,)), dma((NG,)),
        ],
        compiler_params=pltpu.CompilerParams(
            collective_id=0, has_side_effects=True, vmem_limit_bytes=60000 * 1024
        ),
    )(start, jnp.asarray(frequencies()), queries, new_keys, new_values, cache_keys, cache_values)


def solution(mesh):
    placed = (
        P(("head", "kv"), None),
        P(("head", "kv"), None),
        P(("head", "kv"), None),
        P(None, "kv", None),
        P(None, "kv", None),
        P(),
    )
    return jax.shard_map(
        shards, mesh=mesh, in_specs=placed, out_specs=P(("head", "kv"), None), check_vma=False
    )
```

```python
import functools
import math

import jax
import jax.numpy as jnp
import numpy as np
from jax import lax
from jax.experimental import pallas as pl
from jax.experimental.pallas import tpu as pltpu
from jax.sharding import PartitionSpec as P

HEADS = 32
KVH = 8
HD = 128
GROUP = HEADS // KVH
THETA = 500000.0
MESH = pl.DeviceIdType.MESH

NX, NY, NZ, NC = 4, 8, 8, 2
NG = NX * NC
TOK = 4
ROWS = TOK * GROUP
CHUNK = NG * ROWS
EXP_SCALE = HD ** (-0.5) * math.log2(math.e)


def frequencies():
    half = HD // 2
    base = THETA ** (-(np.arange(half, dtype=np.float64) * 2.0 / HD))
    wave = 2.0 * np.pi / base
    smooth = (8192.0 / wave - 1.0) / 3.0
    blended = (1.0 - smooth) * base / 8.0 + smooth * base
    freq = np.where(wave < 2048.0, base, np.where(wave > 8192.0, base / 8.0, blended))
    return np.concatenate([freq, freq]).astype(np.float32)[None, :]


def kernel(
    start_hbm, freq_hbm, q_hbm, k_hbm, v_hbm, ck_ref, cv_ref, o_ref,
    start_ref, freq_ref, q_ref, k_ref, v_ref,
    sq, skv, qall, kvall, kbuf, vbuf, acc, low, tot, so, ss, ro, rs, sf,
    isem, csem, xsend, xrecv, qsend, qrecv, fsend, frecv, osend, orecv, ssend, srecv, rsend, rrecv,
):
    cached = ck_ref.shape[1]
    old = 2 * cached
    fresh = NY * NG * TOK
    head, kv = lax.axis_index("head"), lax.axis_index("kv")
    x, y = lax.div(head, NY), lax.rem(head, NY)
    z, c = lax.div(kv, NC), lax.rem(kv, NC)
    g = x * NC + c

    def of_group(other):
        return (lax.div(other, NC) * NY + y, z * NC + lax.rem(other, NC))

    def of_plane(other):
        return (head, other * NC + c)

    def of_row(other):
        return (x * NY + other, kv)

    groups = [lax.rem(g + i, NG) for i in range(1, NG)]
    planes = [lax.rem(z + i, NZ) for i in (1, 7, 2, 6, 3, 5, 4)]
    rows = [lax.rem(y + i, NY) for i in (4, 3, 5, 2, 6, 1, 7)]

    barrier = pltpu.get_barrier_semaphore()
    peers = [of_group(i) for i in groups] + [of_plane(i) for i in planes] + [of_row(i) for i in rows]
    for peer in peers:
        pl.semaphore_signal(barrier, inc=1, device_id=peer, device_id_type=MESH)

    inputs = [
        pltpu.make_async_copy(source, target, isem.at[i])
        for i, (source, target) in enumerate(
            (
                (start_hbm, start_ref), (freq_hbm, freq_ref), (q_hbm, q_ref), (k_hbm, k_ref),
                (v_hbm, v_ref),
            )
        )
    ]
    for copy in inputs:
        copy.start()
    own_k = pltpu.make_async_copy(ck_ref.at[g], kbuf.at[pl.ds(0, cached)], csem.at[0])
    own_v = pltpu.make_async_copy(cv_ref.at[g], vbuf.at[pl.ds(0, cached)], csem.at[1])
    own_k.start()
    own_v.start()
    for copy in inputs:
        copy.wait()

    first = start_ref[0] + (head * (NZ * NC) + kv) * TOK
    places = first + lax.broadcasted_iota(jnp.int32, (TOK, HD), 0)
    angle = places.astype(jnp.float32) * freq_ref[...]
    lane = lax.broadcasted_iota(jnp.int32, (TOK, HD), 1)
    cosine = jnp.cos(angle)
    sine = jnp.sin(angle)
    sine = jnp.where(lane < HD // 2, -sine, sine)
    cos_q = jnp.concatenate([cosine] * GROUP, 0)
    sin_q = jnp.concatenate([sine] * GROUP, 0)
    for i in range(NG):
        part = jnp.concatenate(
            [
                q_ref[:, (i * GROUP + j) * HD : (i * GROUP + j + 1) * HD].astype(jnp.float32)
                for j in range(GROUP)
            ],
            0,
        )
        turned = part * cos_q + pltpu.roll(part, HD // 2, 1) * sin_q
        sq[i] = turned.astype(jnp.bfloat16)
        part = k_ref[:, i * HD : (i + 1) * HD].astype(jnp.float32)
        turned = part * cosine + pltpu.roll(part, HD // 2, 1) * sine
        value = v_ref[:, i * HD : (i + 1) * HD].astype(jnp.float32)
        skv[i] = jnp.concatenate([turned, value], 0).astype(jnp.bfloat16)

    pl.semaphore_wait(barrier, len(peers))

    sends = []

    def send(source, target, sent, got, device):
        copy = pltpu.make_async_remote_copy(
            src_ref=source, dst_ref=target, send_sem=sent, recv_sem=got,
            device_id=device, device_id_type=MESH,
        )
        copy.start()
        sends.append(copy)

    def landed(target, got):
        pltpu.make_async_copy(target, target, got).wait()

    partner = x * NC + (1 - c)
    for i in groups:
        send(sq.at[i], qall.at[z, g], xsend.at[0, i], xrecv.at[0, g], of_group(i))
    for i in groups:
        send(skv.at[i], kvall.at[y, g], xsend.at[1, i], xrecv.at[1, g], of_group(i))
    for i, (source, target) in enumerate(((ck_ref, kbuf), (cv_ref, vbuf))):
        half = target.at[pl.ds(cached, cached)]
        send(source.at[partner], half, csem.at[2 + i], csem.at[4 + i], of_group(partner))
    qall[z, g] = sq[g]
    kvall[y, g] = skv[g]

    for i in groups:
        landed(qall.at[z, i], xrecv.at[0, i])
    for i in planes:
        send(qall.at[z], qall.at[z], qsend.at[i], qrecv.at[z], of_plane(i))
    for i in groups:
        landed(kvall.at[y, i], xrecv.at[1, i])
    for i in rows:
        send(kvall.at[y], kvall.at[y], fsend.at[i], frecv.at[y], of_row(i))

    own_k.wait()
    own_v.wait()
    for i, target in enumerate((kbuf, vbuf)):
        landed(target.at[pl.ds(cached, cached)], csem.at[4 + i])

    wide = 2 * CHUNK
    square = (CHUNK, CHUNK)
    diagonal = lax.broadcasted_iota(jnp.int32, square, 0) == lax.broadcasted_iota(
        jnp.int32, square, 1
    )

    def pair_of(i):
        return (lax.rem(z - i + NZ, NZ), lax.rem(z + i + 1, NZ))

    def queries_of(pair):
        return jnp.concatenate([qall[one].reshape(CHUNK, HD) for one in pair], 0)

    def scores_of(queries, keys):
        return lax.dot_general(
            queries, keys, (((1,), (1,)), ((), ())), preferred_element_type=jnp.float32
        )

    def weigh(probs, values):
        ones = jnp.ones(values.shape, jnp.bfloat16)
        both = jnp.dot(
            probs, jnp.concatenate([values, ones], 1), preferred_element_type=jnp.float32
        )
        return both[:, :HD], both[:, HD:]

    def await_pair(i, pair):
        @pl.when(i > 0)
        def _():
            landed(qall.at[pair[0]], qrecv.at[pair[0]])

        landed(qall.at[pair[1]], qrecv.at[pair[1]])

    def on_cached(i, carry):
        pair = pair_of(i)
        await_pair(i, pair)
        scores = scores_of(queries_of(pair), kbuf[:old])
        top = jnp.max(scores, 1, keepdims=True) * EXP_SCALE
        probs = jnp.exp2(scores * EXP_SCALE - top).astype(jnp.bfloat16)
        output, total = weigh(probs, vbuf[:old])
        acc[i] = output
        tot[i] = total
        low[i] = jnp.broadcast_to(top, (wide, HD))
        return carry

    lax.fori_loop(0, 2, on_cached, 0)

    for i in rows:
        landed(kvall.at[i], frecv.at[i])
    for i in range(NY):
        for j in range(NG // 4):
            four = [kvall[i, j * 4 + n].astype(jnp.float32) for n in range(4)]
            place = old + (i * NG + j * 4) * TOK
            kbuf[place : place + 16] = jnp.concatenate(
                [one[:TOK] for one in four], 0
            ).astype(jnp.bfloat16)
            vbuf[place : place + 16] = jnp.concatenate(
                [one[TOK:] for one in four], 0
            ).astype(jnp.bfloat16)

    row = lax.broadcasted_iota(jnp.int32, (wide, fresh), 0)
    column = lax.broadcasted_iota(jnp.int32, (wide, fresh), 1)
    row_group = lax.rem(lax.div(row, ROWS), NG)
    row_token = (lax.div(row_group, NC) * NY + y) * (NZ * NC * TOK) + (
        lax.rem(row_group, NC) * TOK + lax.rem(row, TOK)
    )
    column_group = lax.rem(lax.div(column, TOK), NG)
    column_token = (
        lax.div(column_group, NC) * NY + lax.div(column, NG * TOK)
    ) * (NZ * NC * TOK) + (lax.rem(column_group, NC) * TOK + lax.rem(column, TOK))
    behind = row_token - column_token - z * (NC * TOK)

    def hide(scores, pair):
        plane = jnp.where(row < CHUNK, pair[0], pair[1]) * (NC * TOK)
        return jnp.where(behind + plane >= 0, scores, -1e30)

    def give(i, pair, output, total, top):
        level = top + jnp.log2(total)
        output = (output / total).astype(jnp.bfloat16)
        for n in range(2):
            part = slice(n * CHUNK, (n + 1) * CHUNK)
            so[pair[n]] = output[part]
            ss[pair[n]] = jnp.sum(jnp.where(diagonal, level[part], 0.0), 0, keepdims=True)

        def one(other):
            for source, target, sent, got in ((so, ro, osend, orecv), (ss, rs, ssend, srecv)):
                pltpu.make_async_remote_copy(
                    src_ref=source.at[other], dst_ref=target.at[z], send_sem=sent.at[other],
                    recv_sem=got.at[z], device_id=of_plane(other), device_id_type=MESH,
                ).start()

        @pl.when(i > 0)
        def _():
            one(pair[0])

        one(pair[1])

    def on_new(i, carry):
        pair = pair_of(i)
        scores = hide(scores_of(queries_of(pair), kbuf[old:]), pair)
        before = low[i]
        top = jnp.maximum(before, jnp.max(scores, 1, keepdims=True) * EXP_SCALE)
        both = jnp.concatenate([top] * (fresh // HD), 1)
        probs = jnp.exp2(scores * EXP_SCALE - both).astype(jnp.bfloat16)
        output, total = weigh(probs, vbuf[old:])
        keep = jnp.exp2(before - top)
        give(i, pair, acc[i] * keep + output, tot[i] * keep + total, top)
        return carry

    lax.fori_loop(0, 2, on_new, 0)

    def on_all(i, carry):
        pair = pair_of(i)
        await_pair(i, pair)
        scores = scores_of(queries_of(pair), kbuf[...])
        scores = jnp.concatenate([scores[:, :old], hide(scores[:, old:], pair)], 1)
        top = jnp.max(scores, 1, keepdims=True) * EXP_SCALE
        probs = jnp.exp2(scores * EXP_SCALE - top).astype(jnp.bfloat16)
        output, total = weigh(probs, vbuf[...])
        give(i, pair, output, total, top)
        return carry

    lax.fori_loop(2, NZ // 2, on_all, 0)
    ro[z] = so[z]
    rs[z] = ss[z]

    for i in planes:
        landed(rs.at[i], srecv.at[i])
        landed(ro.at[i], orecv.at[i])
    levels = rs[:, 0, :]
    weight = jnp.exp2(levels - jnp.max(levels, 0, keepdims=True))
    weight = weight / jnp.sum(weight, 0, keepdims=True)
    weight = jnp.transpose(weight)
    total = weight[:, 0:1] * ro[0].astype(jnp.float32)
    for i in range(1, NZ):
        total = total + weight[:, i : i + 1] * ro[i].astype(jnp.float32)
    for i in range(NG):
        for j in range(GROUP):
            place = i * ROWS + j * TOK
            sf[i, :, j * HD : (j + 1) * HD] = total[place : place + TOK].astype(jnp.bfloat16)
    width = GROUP * HD
    place = pl.ds(pl.multiple_of(g * width, width), width)
    for i in groups:
        send(sf.at[i], o_ref.at[:, place], rsend.at[i], rrecv.at[g], of_group(i))
    own = pltpu.make_async_copy(sf.at[g], o_ref.at[:, place], rsend.at[g])
    own.start()
    for copy in sends:
        copy.wait_send()
    for i in planes:
        for source, sent in ((so, osend), (ss, ssend)):
            landed(source.at[i], sent.at[i])
    own.wait()
    for i in groups:
        landed(o_ref.at[:, pl.ds(pl.multiple_of(i * width, width), width)], rrecv.at[i])


def shards(queries, new_keys, new_values, cache_keys, cache_values, start):
    cached = cache_keys.shape[1]
    keys = 2 * cached + NY * NG * TOK
    hbm = pl.BlockSpec(memory_space=pltpu.HBM)
    dma = pltpu.SemaphoreType.DMA
    bf16 = jnp.bfloat16
    return pl.pallas_call(
        kernel,
        out_shape=jax.ShapeDtypeStruct((TOK, HEADS * HD), bf16),
        in_specs=[hbm] * 7,
        out_specs=hbm,
        scratch_shapes=[
            pltpu.SMEM((1,), jnp.int32),
            pltpu.VMEM((1, HD), jnp.float32),
            pltpu.VMEM((TOK, HEADS * HD), bf16),
            pltpu.VMEM((TOK, KVH * HD), bf16),
            pltpu.VMEM((TOK, KVH * HD), bf16),
            pltpu.VMEM((NG, ROWS, HD), bf16),
            pltpu.VMEM((NG, 2 * TOK, HD), bf16),
            pltpu.VMEM((NZ, NG, ROWS, HD), bf16),
            pltpu.VMEM((NY, NG, 2 * TOK, HD), bf16),
            pltpu.VMEM((keys, HD), bf16),
            pltpu.VMEM((keys, HD), bf16),
            pltpu.VMEM((2, 2 * CHUNK, HD), jnp.float32),
            pltpu.VMEM((2, 2 * CHUNK, HD), jnp.float32),
            pltpu.VMEM((2, 2 * CHUNK, HD), jnp.float32),
            pltpu.VMEM((NZ, CHUNK, HD), bf16),
            pltpu.VMEM((NZ, 1, CHUNK), jnp.float32),
            pltpu.VMEM((NZ, CHUNK, HD), bf16),
            pltpu.VMEM((NZ, 1, CHUNK), jnp.float32),
            pltpu.VMEM((NG, TOK, GROUP * HD), bf16),
            dma((5,)), dma((6,)), dma((2, NG)), dma((2, NG)), dma((NZ,)), dma((NZ,)), dma((NY,)), dma((NY,)),
            dma((NZ,)), dma((NZ,)), dma((NZ,)), dma((NZ,)), dma((NG,)), dma((NG,)),
        ],
        compiler_params=pltpu.CompilerParams(
            collective_id=0, has_side_effects=True, vmem_limit_bytes=60000 * 1024
        ),
    )(start, jnp.asarray(frequencies()), queries, new_keys, new_values, cache_keys, cache_values)


def solution(mesh):
    placed = (
        P(("head", "kv"), None),
        P(("head", "kv"), None),
        P(("head", "kv"), None),
        P(None, "kv", None),
        P(None, "kv", None),
        P(),
    )
    return jax.shard_map(
        shards, mesh=mesh, in_specs=placed, out_specs=P(("head", "kv"), None), check_vma=False
    )
```

```python
import math

import jax
import jax.numpy as jnp
import numpy as np
from jax import lax
from jax.experimental import pallas as pl
from jax.experimental.pallas import tpu as pltpu
from jax.sharding import PartitionSpec as P

HEADS = 32
KVH = 8
HD = 128
GROUP = HEADS // KVH
THETA = 500000.0
MESH = pl.DeviceIdType.MESH

NX, NY, NZ, NC = 4, 8, 8, 2
NG = NX * NC
NS = NZ * NC
OWN = KVH // NC
TOK = 4
ROWS = TOK * GROUP
ALL = NS * ROWS
FRESH = NY * NG * TOK
EXP_SCALE = HD ** (-0.5) * math.log2(math.e)
ORDER = (0, 1, 7, 2, 6, 3, 5, 4)
PLACE = tuple(ORDER.index(i) for i in range(8))
PIECES = 2
PART = NY // PIECES


def frequencies():
    half = HD // 2
    base = THETA ** (-(np.arange(half, dtype=np.float64) * 2.0 / HD))
    wave = 2.0 * np.pi / base
    smooth = (8192.0 / wave - 1.0) / 3.0
    blended = (1.0 - smooth) * base / 8.0 + smooth * base
    freq = np.where(wave < 2048.0, base, np.where(wave > 8192.0, base / 8.0, blended))
    return np.concatenate([freq, freq]).astype(np.float32)[None, :]


def kernel(
    start_hbm, freq_hbm, q_hbm, k_hbm, v_hbm, ck_ref, cv_ref, o_ref,
    start_ref, freq_ref, q_ref, k_ref, v_ref,
    sq, qall, ybuf, piece, kvb, acc, low, tot, so, ss, ro, rs, turn, out,
    isem, csem, qsend, qrecv, ysend, yrecv, xsend, xrecv, osend, orecv, ssend, srecv,
):
    cached = ck_ref.shape[1]
    old = 2 * cached
    head, kv = lax.axis_index("head"), lax.axis_index("kv")
    x, y = lax.div(head, NY), lax.rem(head, NY)
    z, c = lax.div(kv, NC), lax.rem(kv, NC)
    g = x * NC + c
    mine, theirs = c * OWN, (1 - c) * OWN

    def of_row(other):
        return (lax.div(other, NC) * NY + y, z * NC + lax.rem(other, NC))

    column = [lax.rem(z + d, NZ) * NC + n for d in ORDER[1:] for n in range(NC)]
    partner = z * NC + (1 - c)
    column = [partner] + column
    ring = [lax.rem(y + d, NY) for d in ORDER[1:]]
    row = [lax.rem(g + i, NG) for i in range(1, NG)]

    barrier = pltpu.get_barrier_semaphore()
    peers = (
        [(head, i) for i in column] + [(x * NY + i, kv) for i in ring] + [of_row(i) for i in row]
    )
    for device in peers:
        pl.semaphore_signal(barrier, inc=1, device_id=device, device_id_type=MESH)

    inputs = [
        pltpu.make_async_copy(source, target, isem.at[i])
        for i, (source, target) in enumerate(
            (
                (start_hbm, start_ref), (freq_hbm, freq_ref), (q_hbm, q_ref), (k_hbm, k_ref),
                (v_hbm, v_ref),
            )
        )
    ]
    for copy in inputs:
        copy.start()
    caches = []
    for i, source in enumerate((ck_ref, cv_ref)):
        copy = pltpu.make_async_copy(
            source.at[pl.ds(mine, OWN)], kvb.at[i, :, pl.ds(0, cached)], csem.at[i]
        )
        copy.start()
        caches.append(copy)
    for copy in inputs:
        copy.wait()

    first = start_ref[0] + (head * NS + kv) * TOK
    places = first + lax.broadcasted_iota(jnp.int32, (TOK, HD), 0)
    angle = places.astype(jnp.float32) * freq_ref[...]
    lane = lax.broadcasted_iota(jnp.int32, (TOK, HD), 1)
    cosine = jnp.cos(angle)
    sine = jnp.sin(angle)
    sine = jnp.where(lane < HD // 2, -sine, sine)
    cos_q = jnp.concatenate([cosine] * GROUP, 0)
    sin_q = jnp.concatenate([sine] * GROUP, 0)
    for i in range(KVH):
        part = jnp.concatenate(
            [
                q_ref[:, (i * GROUP + j) * HD : (i * GROUP + j + 1) * HD].astype(jnp.float32)
                for j in range(GROUP)
            ],
            0,
        )
        turned = part * cos_q + pltpu.roll(part, HD // 2, 1) * sin_q
        sq[i] = turned.astype(jnp.bfloat16)
        part = k_ref[:, i * HD : (i + 1) * HD].astype(jnp.float32)
        turned = part * cosine + pltpu.roll(part, HD // 2, 1) * sine
        value = v_ref[:, i * HD : (i + 1) * HD].astype(jnp.float32)
        ybuf[0, i] = jnp.concatenate([turned, value], 0).astype(jnp.bfloat16)

    pl.semaphore_wait(barrier, len(peers))

    sends = []

    def send(source, target, sent, got, device):
        copy = pltpu.make_async_remote_copy(
            src_ref=source, dst_ref=target, send_sem=sent, recv_sem=got,
            device_id=device, device_id_type=MESH,
        )
        copy.start()
        sends.append(copy)

    def landed(target, got):
        pltpu.make_async_copy(target, target, got).wait()

    for i in column:
        half = sq.at[pl.ds(lax.rem(i, NC) * OWN, OWN)]
        send(half, qall.at[:, kv], qsend.at[i], qrecv.at[kv], (head, i))
    for d, i in zip(ORDER[1:], ring):
        place = PLACE[(NY - d) % NY]
        send(ybuf.at[0], ybuf.at[place], ysend.at[place], yrecv.at[place], (x * NY + i, kv))
    for i, source in enumerate((ck_ref, cv_ref)):
        send(
            source.at[pl.ds(theirs, OWN)], kvb.at[i, :, pl.ds(cached, cached)],
            csem.at[2 + i], csem.at[4 + i], (head, partner),
        )
    for j in range(OWN):
        qall[j, kv] = sq[mine + j]

    for m in range(PIECES):
        for i in range(m * PART, (m + 1) * PART):
            if i > 0:
                landed(ybuf.at[i], yrecv.at[i])
        for j in range(KVH):
            four = [ybuf[m * PART + n, j].astype(jnp.float32) for n in range(PART)]
            piece[m, 0, j] = jnp.concatenate([one[:TOK] for one in four], 0).astype(jnp.bfloat16)
            piece[m, 1, j] = jnp.concatenate([one[TOK:] for one in four], 0).astype(jnp.bfloat16)
        size = PART * TOK
        there = pl.ds(pl.multiple_of(old + (g * PIECES + m) * size, size), size)
        for i in row:
            half = piece.at[m, :, pl.ds(lax.rem(i, NC) * OWN, OWN)]
            send(half, kvb.at[:, :, there], xsend.at[m, i], xrecv.at[m, g], of_row(i))
        for j in range(OWN):
            kvb[0, j, there] = piece[m, 0, mine + j]
            kvb[1, j, there] = piece[m, 1, mine + j]

    for i, copy in enumerate(caches):
        copy.wait()
        landed(kvb.at[i, :, pl.ds(cached, cached)], csem.at[4 + i])
    for i in column:
        landed(qall.at[:, i], qrecv.at[i])

    def scores_of(j, keys):
        return lax.dot_general(
            qall[j].reshape(ALL, HD), keys, (((1,), (1,)), ((), ())),
            preferred_element_type=jnp.float32,
        )

    def weigh(probs, values):
        ones = jnp.ones(values.shape, jnp.bfloat16)
        both = jnp.dot(
            probs, jnp.concatenate([values, ones], 1), preferred_element_type=jnp.float32
        )
        return both[:, :HD], both[:, HD:]

    def on_cached(j, carry):
        scores = scores_of(j, kvb[0, j, :old])
        top = jnp.max(scores, 1, keepdims=True) * EXP_SCALE
        probs = jnp.exp2(scores * EXP_SCALE - top).astype(jnp.bfloat16)
        output, total = weigh(probs, kvb[1, j, :old])
        acc[j] = output
        tot[j] = total
        low[j] = jnp.broadcast_to(top, (ALL, HD))
        return carry

    lax.fori_loop(0, OWN, on_cached, 0)

    for m in range(PIECES):
        size = PART * TOK
        for i in row:
            there = pl.ds(pl.multiple_of(old + (i * PIECES + m) * size, size), size)
            landed(kvb.at[:, :, there], xrecv.at[m, i])

    at_row = lax.broadcasted_iota(jnp.int32, (ALL, FRESH), 0)
    at_key = lax.broadcasted_iota(jnp.int32, (ALL, FRESH), 1)
    row_token = (head * NS + lax.div(at_row, ROWS)) * TOK + lax.rem(at_row, TOK)
    source = lax.div(at_key, NY * TOK)
    place = lax.rem(lax.div(at_key, TOK), NY)
    away = lax.div(place + 1, 2)
    away = jnp.where(lax.rem(place, 2) == 1, away, NY - away)
    key_head = lax.div(source, NC) * NY + lax.rem(y + away, NY)
    key_token = (key_head * NS + z * NC + lax.rem(source, NC)) * TOK + lax.rem(at_key, TOK)
    visible = key_token <= row_token
    square = (CHUNK, CHUNK)
    diagonal = lax.broadcasted_iota(jnp.int32, square, 0) == lax.broadcasted_iota(
        jnp.int32, square, 1
    )

    for j in range(OWN):
        scores = jnp.where(visible, scores_of(j, kvb[0, j, old:]), -1e30)
        before = low[j]
        top = jnp.maximum(before, jnp.max(scores, 1, keepdims=True) * EXP_SCALE)
        both = jnp.concatenate([top] * (FRESH // HD), 1)
        probs = jnp.exp2(scores * EXP_SCALE - both).astype(jnp.bfloat16)
        output, total = weigh(probs, kvb[1, j, old:])
        keep = jnp.exp2(before - top)
        output = acc[j] * keep + output
        total = tot[j] * keep + total
        level = top + jnp.log2(total)
        output = (output / total).astype(jnp.bfloat16)
        so[:, j] = output.reshape(NS, ROWS, HD)
        for n in range(HALVES):
            part = level[n * CHUNK : (n + 1) * CHUNK]
            ss[n, j : j + 1, :] = jnp.sum(jnp.where(diagonal, part, 0.0), 0, keepdims=True)
        if j % 2 == 1:
            two = pl.ds(j - 1, 2)
            for i in column:
                send(
                    so.at[i, two], ro.at[kv, two], osend.at[j // 2, i], orecv.at[j // 2, kv],
                    (head, i),
                )
    for i in column:
        send(ss.at[lax.div(i, NS // HALVES)], rs.at[kv], ssend.at[i], srecv.at[kv], (head, i))
    ro[kv] = so[kv]
    rs[kv] = ss[lax.div(kv, NS // HALVES)]

    for i in column:
        landed(rs.at[i], srecv.at[i])
    levels = jnp.concatenate(
        [rs[:, j : j + 1, :].reshape(NZ, NC, CHUNK) for j in range(OWN)], 1
    )
    weight = jnp.exp2(levels - jnp.max(levels, 0, keepdims=True))
    weight = weight / jnp.sum(weight, 0, keepdims=True)
    turn[...] = jnp.transpose(weight.reshape(NZ * KVH, CHUNK))
    begin = pl.multiple_of(lax.rem(kv, NS // HALVES) * ROWS, ROWS)
    weight = turn[pl.ds(begin, ROWS), :]
    for i in column:
        for m in range(OWN // 2):
            two = pl.ds(2 * m, 2)
            landed(ro.at[i, two], orecv.at[m, i])
    for n in range(NC):
        for j in range(OWN):
            total = jnp.zeros((ROWS, HD), jnp.float32)
            for i in range(NZ):
                at = i * KVH + j * NC + n
                total = total + weight[:, at : at + 1] * ro[i * NC + n, j].astype(jnp.float32)
            for h in range(GROUP):
                at = ((n * OWN + j) * GROUP + h) * HD
                out[:, at : at + HD] = total[h * TOK : (h + 1) * TOK].astype(jnp.bfloat16)
    done = pltpu.make_async_copy(out, o_ref, isem.at[0])
    done.start()
    for copy in sends:
        copy.wait_send()
    done.wait()


HALVES = 2
CHUNK = ALL // HALVES


def shards(queries, new_keys, new_values, cache_keys, cache_values, start):
    keys = 2 * cache_keys.shape[1] + FRESH
    hbm = pl.BlockSpec(memory_space=pltpu.HBM)
    dma = pltpu.SemaphoreType.DMA
    bf16 = jnp.bfloat16
    f32 = jnp.float32
    return pl.pallas_call(
        kernel,
        out_shape=jax.ShapeDtypeStruct((TOK, HEADS * HD), bf16),
        in_specs=[hbm] * 7,
        out_specs=hbm,
        scratch_shapes=[
            pltpu.SMEM((1,), jnp.int32),
            pltpu.VMEM((1, HD), f32),
            pltpu.VMEM((TOK, HEADS * HD), bf16),
            pltpu.VMEM((TOK, KVH * HD), bf16),
            pltpu.VMEM((TOK, KVH * HD), bf16),
            pltpu.VMEM((KVH, ROWS, HD), bf16),
            pltpu.VMEM((OWN, NS, ROWS, HD), bf16),
            pltpu.VMEM((NY, KVH, 2 * TOK, HD), bf16),
            pltpu.VMEM((PIECES, 2, KVH, PART * TOK, HD), bf16),
            pltpu.VMEM((2, OWN, keys, HD), bf16),
            pltpu.VMEM((OWN, ALL, HD), f32),
            pltpu.VMEM((OWN, ALL, HD), f32),
            pltpu.VMEM((OWN, ALL, HD), f32),
            pltpu.VMEM((NS, OWN, ROWS, HD), bf16),
            pltpu.VMEM((HALVES, OWN, CHUNK), f32),
            pltpu.VMEM((NS, OWN, ROWS, HD), bf16),
            pltpu.VMEM((NS, OWN, CHUNK), f32),
            pltpu.VMEM((CHUNK, NZ * KVH), f32),
            pltpu.VMEM((TOK, HEADS * HD), bf16),
            dma((5,)), dma((6,)), dma((NS,)), dma((NS,)), dma((NY,)), dma((NY,)),
            dma((PIECES, NG)), dma((PIECES, NG)), dma((2, NS)), dma((2, NS)), dma((NS,)), dma((NS,)),
        ],
        compiler_params=pltpu.CompilerParams(
            collective_id=0, has_side_effects=True, vmem_limit_bytes=60000 * 1024
        ),
    )(start, jnp.asarray(frequencies()), queries, new_keys, new_values, cache_keys, cache_values)


def solution(mesh):
    placed = (
        P(("head", "kv"), None),
        P(("head", "kv"), None),
        P(("head", "kv"), None),
        P(None, "kv", None),
        P(None, "kv", None),
        P(),
    )
    return jax.shard_map(
        shards, mesh=mesh, in_specs=placed, out_specs=P(("head", "kv"), None), check_vma=False
    )
```

```python
import math

import jax
import jax.numpy as jnp
import numpy as np
from jax import lax
from jax.experimental import pallas as pl
from jax.experimental.pallas import tpu as pltpu
from jax.sharding import PartitionSpec as P

HEADS = 32
KVH = 8
HD = 128
GROUP = HEADS // KVH
THETA = 500000.0
MESH = pl.DeviceIdType.MESH

NX, NY, NZ, NC = 4, 8, 8, 2
NG = NX * NC
NS = NZ * NC
OWN = KVH // NC
TOK = 4
ROWS = TOK * GROUP
ALL = NS * ROWS
FRESH = NY * NG * TOK
EXP_SCALE = HD ** (-0.5) * math.log2(math.e)
ORDER = (0, 1, 7, 2, 6, 3, 5, 4)
PLACE = tuple(ORDER.index(i) for i in range(8))
PIECES = 2
PART = NY // PIECES
PAIR = 2


def frequencies():
    half = HD // 2
    base = THETA ** (-(np.arange(half, dtype=np.float64) * 2.0 / HD))
    wave = 2.0 * np.pi / base
    smooth = (8192.0 / wave - 1.0) / 3.0
    blended = (1.0 - smooth) * base / 8.0 + smooth * base
    freq = np.where(wave < 2048.0, base, np.where(wave > 8192.0, base / 8.0, blended))
    return np.concatenate([freq, freq]).astype(np.float32)[None, :]


def kernel(
    start_hbm, freq_hbm, q_hbm, k_hbm, v_hbm, ck_ref, cv_ref, o_ref,
    start_ref, freq_ref, q_ref, k_ref, v_ref,
    sq, qall, ybuf, piece, kvb, acc, low, tot, so, ss, ro, rs, out,
    isem, csem, qsend, qrecv, ysend, yrecv, xsend, xrecv, osend, orecv, ssend, srecv,
):
    cached = ck_ref.shape[1]
    old = 2 * cached
    head, kv = lax.axis_index("head"), lax.axis_index("kv")
    x, y = lax.div(head, NY), lax.rem(head, NY)
    z, c = lax.div(kv, NC), lax.rem(kv, NC)
    g = x * NC + c
    mine, theirs = c * OWN, (1 - c) * OWN

    def of_row(other):
        return (lax.div(other, NC) * NY + y, z * NC + lax.rem(other, NC))

    column = [lax.rem(z + d, NZ) * NC + n for d in ORDER[1:] for n in range(NC)]
    partner = z * NC + (1 - c)
    column = [partner] + column
    ring = [lax.rem(y + d, NY) for d in ORDER[1:]]
    row = [lax.rem(g + i, NG) for i in range(1, NG)]
    back = column[::-1]

    barrier = pltpu.get_barrier_semaphore()
    peers = (
        [(head, i) for i in column] + [(x * NY + i, kv) for i in ring] + [of_row(i) for i in row]
    )
    for device in peers:
        pl.semaphore_signal(barrier, inc=1, device_id=device, device_id_type=MESH)

    inputs = [
        pltpu.make_async_copy(source, target, isem.at[i])
        for i, (source, target) in enumerate(
            (
                (start_hbm, start_ref), (freq_hbm, freq_ref), (q_hbm, q_ref), (k_hbm, k_ref),
                (v_hbm, v_ref),
            )
        )
    ]
    for copy in inputs:
        copy.start()
    caches = []
    for i, source in enumerate((ck_ref, cv_ref)):
        copy = pltpu.make_async_copy(
            source.at[pl.ds(mine, OWN)], kvb.at[i, :, pl.ds(0, cached)], csem.at[i]
        )
        copy.start()
        caches.append(copy)
    for copy in inputs:
        copy.wait()

    first = start_ref[0] + (head * NS + kv) * TOK
    places = first + lax.broadcasted_iota(jnp.int32, (TOK, HD), 0)
    angle = places.astype(jnp.float32) * freq_ref[...]
    lane = lax.broadcasted_iota(jnp.int32, (TOK, HD), 1)
    cosine = jnp.cos(angle)
    sine = jnp.sin(angle)
    sine = jnp.where(lane < HD // 2, -sine, sine)
    cos_q = jnp.concatenate([cosine] * GROUP, 0)
    sin_q = jnp.concatenate([sine] * GROUP, 0)
    for i in range(KVH):
        part = jnp.concatenate(
            [
                q_ref[:, (i * GROUP + j) * HD : (i * GROUP + j + 1) * HD].astype(jnp.float32)
                for j in range(GROUP)
            ],
            0,
        )
        turned = part * cos_q + pltpu.roll(part, HD // 2, 1) * sin_q
        sq[i] = turned.astype(jnp.bfloat16)
        part = k_ref[:, i * HD : (i + 1) * HD].astype(jnp.float32)
        turned = part * cosine + pltpu.roll(part, HD // 2, 1) * sine
        value = v_ref[:, i * HD : (i + 1) * HD].astype(jnp.float32)
        ybuf[0, i] = jnp.concatenate([turned, value], 0).astype(jnp.bfloat16)

    pl.semaphore_wait(barrier, len(peers))

    sends = []

    def send(source, target, sent, got, device):
        copy = pltpu.make_async_remote_copy(
            src_ref=source, dst_ref=target, send_sem=sent, recv_sem=got,
            device_id=device, device_id_type=MESH,
        )
        copy.start()
        sends.append(copy)

    def landed(target, got):
        pltpu.make_async_copy(target, target, got).wait()

    for i in column:
        half = sq.at[pl.ds(lax.rem(i, NC) * OWN, OWN)]
        send(half, qall.at[:, kv], qsend.at[i], qrecv.at[kv], (head, i))
    for d, i in zip(ORDER[1:], ring):
        place = PLACE[(NY - d) % NY]
        send(ybuf.at[0], ybuf.at[place], ysend.at[place], yrecv.at[place], (x * NY + i, kv))
    for i, source in enumerate((ck_ref, cv_ref)):
        send(
            source.at[pl.ds(theirs, OWN)], kvb.at[i, :, pl.ds(cached, cached)],
            csem.at[2 + i], csem.at[4 + i], (head, partner),
        )
    for j in range(OWN):
        qall[j, kv] = sq[mine + j]

    size = PART * TOK

    def gather(m):
        for i in range(m * PART, (m + 1) * PART):
            if i > 0:
                landed(ybuf.at[i], yrecv.at[i])
        for j in range(KVH):
            four = [ybuf[m * PART + n, j].astype(jnp.float32) for n in range(PART)]
            piece[m, 0, j] = jnp.concatenate([one[:TOK] for one in four], 0).astype(jnp.bfloat16)
            piece[m, 1, j] = jnp.concatenate([one[TOK:] for one in four], 0).astype(jnp.bfloat16)

    def rows_of(i, m):
        return pl.ds(pl.multiple_of(old + (i * PIECES + m) * size, size), size)

    def forward(h, m):
        two = pl.ds(h * PAIR, PAIR)
        for i in row:
            half = piece.at[m, :, pl.ds(lax.rem(i, NC) * OWN + h * PAIR, PAIR)]
            send(half, kvb.at[:, two, rows_of(g, m)], xsend.at[h, m, i], xrecv.at[h, m, g], of_row(i))
        for j in range(h * PAIR, (h + 1) * PAIR):
            for n in range(2):
                kvb[n, j, rows_of(g, m)] = piece[m, n, mine + j]

    gather(0)
    forward(0, 0)
    gather(1)
    forward(0, 1)
    forward(1, 0)
    forward(1, 1)

    for i, copy in enumerate(caches):
        copy.wait()
        landed(kvb.at[i, :, pl.ds(cached, cached)], csem.at[4 + i])
    for i in column:
        landed(qall.at[:, i], qrecv.at[i])

    def scores_of(j, keys):
        return lax.dot_general(
            qall[j].reshape(ALL, HD), keys, (((1,), (1,)), ((), ())),
            preferred_element_type=jnp.float32,
        )

    def weigh(probs, values):
        ones = jnp.ones(values.shape, jnp.bfloat16)
        both = jnp.dot(
            probs, jnp.concatenate([values, ones], 1), preferred_element_type=jnp.float32
        )
        return both[:, :HD], both[:, HD:]

    def on_cached(j, carry):
        scores = scores_of(j, kvb[0, j, :old])
        top = jnp.max(scores, 1, keepdims=True) * EXP_SCALE
        probs = jnp.exp2(scores * EXP_SCALE - top).astype(jnp.bfloat16)
        output, total = weigh(probs, kvb[1, j, :old])
        acc[j] = output
        tot[j] = total
        low[j] = jnp.broadcast_to(top, (ALL, HD))
        return carry

    at_row = lax.broadcasted_iota(jnp.int32, (ALL, FRESH), 0)
    at_key = lax.broadcasted_iota(jnp.int32, (ALL, FRESH), 1)
    row_token = (head * NS + lax.div(at_row, ROWS)) * TOK + lax.rem(at_row, TOK)
    source = lax.div(at_key, NY * TOK)
    place = lax.rem(lax.div(at_key, TOK), NY)
    away = lax.div(place + 1, 2)
    away = jnp.where(lax.rem(place, 2) == 1, away, NY - away)
    key_head = lax.div(source, NC) * NY + lax.rem(y + away, NY)
    key_token = (key_head * NS + z * NC + lax.rem(source, NC)) * TOK + lax.rem(at_key, TOK)
    visible = key_token <= row_token
    lane_row = lax.broadcasted_iota(jnp.int32, (ALL, HD), 1) - lax.rem(
        lax.broadcasted_iota(jnp.int32, (ALL, HD), 0), ROWS
    )

    ss[...] = jnp.zeros_like(ss)
    for h in range(OWN // PAIR):
        lax.fori_loop(h * PAIR, (h + 1) * PAIR, on_cached, 0)
        two = pl.ds(h * PAIR, PAIR)
        for m in range(PIECES):
            for i in row:
                landed(kvb.at[:, two, rows_of(i, m)], xrecv.at[h, m, i])
        for j in range(h * PAIR, (h + 1) * PAIR):
            scores = jnp.where(visible, scores_of(j, kvb[0, j, old:]), -1e30)
            before = low[j]
            top = jnp.maximum(before, jnp.max(scores, 1, keepdims=True) * EXP_SCALE)
            both = jnp.concatenate([top] * (FRESH // HD), 1)
            probs = jnp.exp2(scores * EXP_SCALE - both).astype(jnp.bfloat16)
            output, total = weigh(probs, kvb[1, j, old:])
            keep = jnp.exp2(before - top)
            output = acc[j] * keep + output
            total = tot[j] * keep + total
            level = top + jnp.log2(total)
            output = (output / total).astype(jnp.bfloat16)
            so[:, j] = output.reshape(NS, ROWS, HD)
            level = jnp.where(lane_row == j * ROWS, level, 0.0).reshape(NS, ROWS, HD)
            ss[...] += jnp.sum(level, 1, keepdims=True)
        for i in back:
            send(so.at[i, two], ro.at[kv, two], osend.at[h, i], orecv.at[h, kv], (head, i))
    for i in back:
        send(ss.at[i], rs.at[kv], ssend.at[i], srecv.at[kv], (head, i))
    ro[kv] = so[kv]
    rs[kv] = ss[kv]

    for i in column:
        landed(rs.at[i], srecv.at[i])
    levels = rs[:, 0, :].reshape(NZ, NC, HD)
    weight = jnp.exp2(levels - jnp.max(levels, 0, keepdims=True))
    weight = weight / jnp.sum(weight, 0, keepdims=True)
    weight = jnp.transpose(weight.reshape(NS, HD))
    for i in column:
        for m in range(OWN // PAIR):
            two = pl.ds(m * PAIR, PAIR)
            landed(ro.at[i, two], orecv.at[m, i])
    for n in range(NC):
        for j in range(OWN):
            total = jnp.zeros((ROWS, HD), jnp.float32)
            for i in range(NZ):
                at = i * NC + n
                share = weight[j * ROWS : (j + 1) * ROWS, at : at + 1]
                total = total + share * ro[at, j].astype(jnp.float32)
            for h in range(GROUP):
                at = ((n * OWN + j) * GROUP + h) * HD
                out[:, at : at + HD] = total[h * TOK : (h + 1) * TOK].astype(jnp.bfloat16)
    done = pltpu.make_async_copy(out, o_ref, isem.at[0])
    done.start()
    for copy in sends:
        copy.wait_send()
    done.wait()


def shards(queries, new_keys, new_values, cache_keys, cache_values, start):
    keys = 2 * cache_keys.shape[1] + FRESH
    hbm = pl.BlockSpec(memory_space=pltpu.HBM)
    dma = pltpu.SemaphoreType.DMA
    bf16 = jnp.bfloat16
    f32 = jnp.float32
    return pl.pallas_call(
        kernel,
        out_shape=jax.ShapeDtypeStruct((TOK, HEADS * HD), bf16),
        in_specs=[hbm] * 7,
        out_specs=pl.BlockSpec(memory_space=pl.ANY),
        scratch_shapes=[
            pltpu.SMEM((1,), jnp.int32),
            pltpu.VMEM((1, HD), f32),
            pltpu.VMEM((TOK, HEADS * HD), bf16),
            pltpu.VMEM((TOK, KVH * HD), bf16),
            pltpu.VMEM((TOK, KVH * HD), bf16),
            pltpu.VMEM((KVH, ROWS, HD), bf16),
            pltpu.VMEM((OWN, NS, ROWS, HD), bf16),
            pltpu.VMEM((NY, KVH, 2 * TOK, HD), bf16),
            pltpu.VMEM((PIECES, 2, KVH, PART * TOK, HD), bf16),
            pltpu.VMEM((2, OWN, keys, HD), bf16),
            pltpu.VMEM((OWN, ALL, HD), f32),
            pltpu.VMEM((OWN, ALL, HD), f32),
            pltpu.VMEM((OWN, ALL, HD), f32),
            pltpu.VMEM((NS, OWN, ROWS, HD), bf16),
            pltpu.VMEM((NS, 1, HD), f32),
            pltpu.VMEM((NS, OWN, ROWS, HD), bf16),
            pltpu.VMEM((NS, 1, HD), f32),
            pltpu.VMEM((TOK, HEADS * HD), bf16),
            dma((5,)), dma((6,)), dma((NS,)), dma((NS,)), dma((NY,)), dma((NY,)),
            dma((2, PIECES, NG)), dma((2, PIECES, NG)), dma((2, NS)), dma((2, NS)), dma((NS,)), dma((NS,)),
        ],
        compiler_params=pltpu.CompilerParams(
            collective_id=0, has_side_effects=True, vmem_limit_bytes=40000 * 1024
        ),
    )(
        start,
        *[
            pltpu.with_memory_space_constraint(one, pltpu.HBM)
            for one in (
                jnp.asarray(frequencies()), queries, new_keys, new_values, cache_keys, cache_values
            )
        ],
    )


def solution(mesh):
    placed = (
        P(("head", "kv"), None),
        P(("head", "kv"), None),
        P(("head", "kv"), None),
        P(None, "kv", None),
        P(None, "kv", None),
        P(),
    )
    return jax.shard_map(
        shards, mesh=mesh, in_specs=placed, out_specs=P(("head", "kv"), None), check_vma=False
    )
```

```python
import math

import jax
import jax.numpy as jnp
import numpy as np
from jax import lax
from jax.experimental import pallas as pl
from jax.experimental.pallas import tpu as pltpu
from jax.sharding import PartitionSpec as P

HEADS = 32
KVH = 8
HD = 128
GROUP = HEADS // KVH
THETA = 500000.0
MESH = pl.DeviceIdType.MESH

NX, NY, NZ, NC = 4, 8, 8, 2
NG = NX * NC
NS = NZ * NC
OWN = KVH // NC
TOK = 4
ROWS = TOK * GROUP
ALL = NS * ROWS
FRESH = NY * NG * TOK
EXP_SCALE = HD ** (-0.5) * math.log2(math.e)
ORDER = (0, 1, 7, 2, 6, 3, 5, 4)
PLACE = tuple(ORDER.index(i) for i in range(8))
PIECES = 2
BLOCKS = 4
PART = NY // PIECES
PAIR = 2


def frequencies():
    half = HD // 2
    base = THETA ** (-(np.arange(half, dtype=np.float64) * 2.0 / HD))
    wave = 2.0 * np.pi / base
    smooth = (8192.0 / wave - 1.0) / 3.0
    blended = (1.0 - smooth) * base / 8.0 + smooth * base
    freq = np.where(wave < 2048.0, base, np.where(wave > 8192.0, base / 8.0, blended))
    return np.concatenate([freq, freq]).astype(np.float32)[None, :]


def kernel(
    start_hbm, freq_hbm, q_hbm, k_hbm, v_hbm, ck_ref, cv_ref, o_ref,
    start_ref, freq_ref, q_ref, k_ref, v_ref,
    sq, qall, ybuf, piece, kvb, acc, low, tot, so, ss, ro, rs, out,
    isem, csem, qsend, qrecv, ysend, yrecv, xsend, xrecv, osend, orecv, ssend, srecv,
):
    cached = ck_ref.shape[1]
    old = 2 * cached
    head, kv = lax.axis_index("head"), lax.axis_index("kv")
    x, y = lax.div(head, NY), lax.rem(head, NY)
    z, c = lax.div(kv, NC), lax.rem(kv, NC)
    g = x * NC + c
    mine, theirs = c * OWN, (1 - c) * OWN

    def of_row(other):
        return (lax.div(other, NC) * NY + y, z * NC + lax.rem(other, NC))

    column = [lax.rem(z + d, NZ) * NC + n for d in ORDER[1:] for n in range(NC)]
    partner = z * NC + (1 - c)
    column = [partner] + column
    ring = [lax.rem(y + d, NY) for d in ORDER[1:]]
    row = [lax.rem(g + i, NG) for i in range(1, NG)]
    back = column[::-1]

    barrier = pltpu.get_barrier_semaphore()
    peers = (
        [(head, i) for i in column] + [(x * NY + i, kv) for i in ring] + [of_row(i) for i in row]
    )
    for device in peers:
        pl.semaphore_signal(barrier, inc=1, device_id=device, device_id_type=MESH)

    inputs = [
        pltpu.make_async_copy(source, target, isem.at[i])
        for i, (source, target) in enumerate(
            (
                (start_hbm, start_ref), (freq_hbm, freq_ref), (q_hbm, q_ref), (k_hbm, k_ref),
                (v_hbm, v_ref),
            )
        )
    ]
    for copy in inputs:
        copy.start()
    caches = []
    for i, source in enumerate((ck_ref, cv_ref)):
        copy = pltpu.make_async_copy(
            source.at[pl.ds(mine, OWN)], kvb.at[i, :, pl.ds(0, cached)], csem.at[i]
        )
        copy.start()
        caches.append(copy)
    for copy in inputs:
        copy.wait()

    first = start_ref[0] + (head * NS + kv) * TOK
    places = first + lax.broadcasted_iota(jnp.int32, (TOK, HD), 0)
    angle = places.astype(jnp.float32) * freq_ref[...]
    lane = lax.broadcasted_iota(jnp.int32, (TOK, HD), 1)
    cosine = jnp.cos(angle)
    sine = jnp.sin(angle)
    sine = jnp.where(lane < HD // 2, -sine, sine)
    cos_q = jnp.concatenate([cosine] * GROUP, 0)
    sin_q = jnp.concatenate([sine] * GROUP, 0)
    for i in range(KVH):
        part = jnp.concatenate(
            [
                q_ref[:, (i * GROUP + j) * HD : (i * GROUP + j + 1) * HD].astype(jnp.float32)
                for j in range(GROUP)
            ],
            0,
        )
        turned = part * cos_q + pltpu.roll(part, HD // 2, 1) * sin_q
        sq[i] = turned.astype(jnp.bfloat16)
        part = k_ref[:, i * HD : (i + 1) * HD].astype(jnp.float32)
        turned = part * cosine + pltpu.roll(part, HD // 2, 1) * sine
        value = v_ref[:, i * HD : (i + 1) * HD].astype(jnp.float32)
        ybuf[0, i] = jnp.concatenate([turned, value], 0).astype(jnp.bfloat16)

    pl.semaphore_wait(barrier, len(peers))

    sends = []

    def send(source, target, sent, got, device):
        copy = pltpu.make_async_remote_copy(
            src_ref=source, dst_ref=target, send_sem=sent, recv_sem=got,
            device_id=device, device_id_type=MESH,
        )
        copy.start()
        sends.append(copy)

    def landed(target, got):
        pltpu.make_async_copy(target, target, got).wait()

    def spread(h):
        for i in column:
            half = sq.at[pl.ds(lax.rem(i, NC) * OWN + h * PAIR, PAIR)]
            target = qall.at[pl.ds(h * PAIR, PAIR), kv]
            send(half, target, qsend.at[h, i], qrecv.at[h, kv], (head, i))

    spread(0)
    for d, i in zip(ORDER[1:], ring):
        place = PLACE[(NY - d) % NY]
        send(ybuf.at[0], ybuf.at[place], ysend.at[place], yrecv.at[place], (x * NY + i, kv))
    spread(1)
    for i, source in enumerate((ck_ref, cv_ref)):
        send(
            source.at[pl.ds(theirs, OWN)], kvb.at[i, :, pl.ds(cached, cached)],
            csem.at[2 + i], csem.at[4 + i], (head, partner),
        )
    for j in range(OWN):
        qall[j, kv] = sq[mine + j]

    size = PART * TOK

    def gather(m):
        for i in range(m * PART, (m + 1) * PART):
            if i > 0:
                landed(ybuf.at[i], yrecv.at[i])
        for j in range(KVH):
            four = [ybuf[m * PART + n, j].astype(jnp.float32) for n in range(PART)]
            piece[m, 0, j] = jnp.concatenate([one[:TOK] for one in four], 0).astype(jnp.bfloat16)
            piece[m, 1, j] = jnp.concatenate([one[TOK:] for one in four], 0).astype(jnp.bfloat16)

    def rows_of(i, m):
        return pl.ds(pl.multiple_of(old + (i * PIECES + m) * size, size), size)

    def forward(h, m):
        two = pl.ds(h * PAIR, PAIR)
        for i in row:
            half = piece.at[m, :, pl.ds(lax.rem(i, NC) * OWN + h * PAIR, PAIR)]
            send(half, kvb.at[:, two, rows_of(g, m)], xsend.at[h, m, i], xrecv.at[h, m, g], of_row(i))
        for j in range(h * PAIR, (h + 1) * PAIR):
            for n in range(2):
                kvb[n, j, rows_of(g, m)] = piece[m, n, mine + j]

    gather(0)
    forward(0, 0)
    gather(1)
    forward(0, 1)
    forward(1, 0)
    forward(1, 1)

    for i, copy in enumerate(caches):
        copy.wait()
        landed(kvb.at[i, :, pl.ds(cached, cached)], csem.at[4 + i])

    def scores_of(j, keys):
        return lax.dot_general(
            qall[j].reshape(ALL, HD), keys, (((1,), (1,)), ((), ())),
            preferred_element_type=jnp.float32,
        )

    def weigh(probs, values):
        ones = jnp.ones(values.shape, jnp.bfloat16)
        both = jnp.dot(
            probs, jnp.concatenate([values, ones], 1), preferred_element_type=jnp.float32
        )
        return both[:, :HD], both[:, HD:]

    def on_cached(j, carry):
        block = old // BLOCKS
        top = output = total = None
        for n in range(BLOCKS):
            keys = slice(n * block, (n + 1) * block)
            scores = scores_of(j, kvb[0, j, keys])
            here = jnp.broadcast_to(jnp.max(scores, 1, keepdims=True) * EXP_SCALE, (ALL, HD))
            peak = here if n == 0 else jnp.maximum(top, here)
            wide = jnp.concatenate([peak] * (block // HD), 1)
            probs = jnp.exp2(scores * EXP_SCALE - wide).astype(jnp.bfloat16)
            added, summed = weigh(probs, kvb[1, j, keys])
            if n == 0:
                output, total = added, summed
            else:
                keep = jnp.exp2(top - peak)
                output = output * keep + added
                total = total * keep + summed
            top = peak
        acc[j] = output
        tot[j] = total
        low[j] = top
        return carry

    at_row = lax.broadcasted_iota(jnp.int32, (ALL, FRESH), 0)
    at_key = lax.broadcasted_iota(jnp.int32, (ALL, FRESH), 1)
    row_token = (head * NS + lax.div(at_row, ROWS)) * TOK + lax.rem(at_row, TOK)
    source = lax.div(at_key, NY * TOK)
    place = lax.rem(lax.div(at_key, TOK), NY)
    away = lax.div(place + 1, 2)
    away = jnp.where(lax.rem(place, 2) == 1, away, NY - away)
    key_head = lax.div(source, NC) * NY + lax.rem(y + away, NY)
    key_token = (key_head * NS + z * NC + lax.rem(source, NC)) * TOK + lax.rem(at_key, TOK)
    visible = key_token <= row_token
    lane_row = lax.broadcasted_iota(jnp.int32, (ALL, HD), 1) - lax.rem(
        lax.broadcasted_iota(jnp.int32, (ALL, HD), 0), ROWS
    )

    ss[...] = jnp.zeros_like(ss)
    for h in range(OWN // PAIR):
        two = pl.ds(h * PAIR, PAIR)
        for i in column:
            landed(qall.at[two, i], qrecv.at[h, i])
        lax.fori_loop(h * PAIR, (h + 1) * PAIR, on_cached, 0, unroll=True)
        for m in range(PIECES):
            for i in row:
                landed(kvb.at[:, two, rows_of(i, m)], xrecv.at[h, m, i])
        for j in range(h * PAIR, (h + 1) * PAIR):
            scores = jnp.where(visible, scores_of(j, kvb[0, j, old:]), -1e30)
            before = low[j]
            top = jnp.maximum(before, jnp.max(scores, 1, keepdims=True) * EXP_SCALE)
            both = jnp.concatenate([top] * (FRESH // HD), 1)
            probs = jnp.exp2(scores * EXP_SCALE - both).astype(jnp.bfloat16)
            output, total = weigh(probs, kvb[1, j, old:])
            keep = jnp.exp2(before - top)
            output = acc[j] * keep + output
            total = tot[j] * keep + total
            level = top + jnp.log2(total)
            output = (output / total).astype(jnp.bfloat16)
            so[:, j] = output.reshape(NS, ROWS, HD)
            level = jnp.where(lane_row == j * ROWS, level, 0.0).reshape(NS, ROWS, HD)
            ss[...] += jnp.sum(level, 1, keepdims=True)
        for i in back:
            send(so.at[i, two], ro.at[kv, two], osend.at[h, i], orecv.at[h, kv], (head, i))
            if h == OWN // PAIR - 1:
                send(ss.at[i], rs.at[kv], ssend.at[i], srecv.at[kv], (head, i))
    ro[kv] = so[kv]
    rs[kv] = ss[kv]

    for i in column:
        landed(rs.at[i], srecv.at[i])
    levels = rs[:, 0, :].reshape(NZ, NC, HD)
    weight = jnp.exp2(levels - jnp.max(levels, 0, keepdims=True))
    weight = weight / jnp.sum(weight, 0, keepdims=True)
    weight = jnp.transpose(weight.reshape(NS, HD))
    for i in column:
        for m in range(OWN // PAIR):
            two = pl.ds(m * PAIR, PAIR)
            landed(ro.at[i, two], orecv.at[m, i])
    for n in range(NC):
        for j in range(OWN):
            total = jnp.zeros((ROWS, HD), jnp.float32)
            for i in range(NZ):
                at = i * NC + n
                share = weight[j * ROWS : (j + 1) * ROWS, at : at + 1]
                total = total + share * ro[at, j].astype(jnp.float32)
            for h in range(GROUP):
                at = ((n * OWN + j) * GROUP + h) * HD
                out[:, at : at + HD] = total[h * TOK : (h + 1) * TOK].astype(jnp.bfloat16)
    done = pltpu.make_async_copy(out, o_ref, isem.at[0])
    done.start()
    for copy in sends:
        copy.wait_send()
    done.wait()


def shards(queries, new_keys, new_values, cache_keys, cache_values, start):
    keys = 2 * cache_keys.shape[1] + FRESH
    hbm = pl.BlockSpec(memory_space=pltpu.HBM)
    dma = pltpu.SemaphoreType.DMA
    bf16 = jnp.bfloat16
    f32 = jnp.float32
    return pl.pallas_call(
        kernel,
        out_shape=jax.ShapeDtypeStruct((TOK, HEADS * HD), bf16),
        in_specs=[hbm] * 7,
        out_specs=pl.BlockSpec(memory_space=pl.ANY),
        scratch_shapes=[
            pltpu.SMEM((1,), jnp.int32),
            pltpu.VMEM((1, HD), f32),
            pltpu.VMEM((TOK, HEADS * HD), bf16),
            pltpu.VMEM((TOK, KVH * HD), bf16),
            pltpu.VMEM((TOK, KVH * HD), bf16),
            pltpu.VMEM((KVH, ROWS, HD), bf16),
            pltpu.VMEM((OWN, NS, ROWS, HD), bf16),
            pltpu.VMEM((NY, KVH, 2 * TOK, HD), bf16),
            pltpu.VMEM((PIECES, 2, KVH, PART * TOK, HD), bf16),
            pltpu.VMEM((2, OWN, keys, HD), bf16),
            pltpu.VMEM((OWN, ALL, HD), f32),
            pltpu.VMEM((OWN, ALL, HD), f32),
            pltpu.VMEM((OWN, ALL, HD), f32),
            pltpu.VMEM((NS, OWN, ROWS, HD), bf16),
            pltpu.VMEM((NS, 1, HD), f32),
            pltpu.VMEM((NS, OWN, ROWS, HD), bf16),
            pltpu.VMEM((NS, 1, HD), f32),
            pltpu.VMEM((TOK, HEADS * HD), bf16),
            dma((5,)), dma((6,)), dma((2, NS)), dma((2, NS)), dma((NY,)), dma((NY,)),
            dma((2, PIECES, NG)), dma((2, PIECES, NG)), dma((2, NS)), dma((2, NS)), dma((NS,)), dma((NS,)),
        ],
        compiler_params=pltpu.CompilerParams(
            collective_id=0, has_side_effects=True, vmem_limit_bytes=40000 * 1024
        ),
    )(
        start,
        *[
            pltpu.with_memory_space_constraint(one, pltpu.HBM)
            for one in (
                jnp.asarray(frequencies()), queries, new_keys, new_values, cache_keys, cache_values
            )
        ],
    )


def solution(mesh):
    placed = (
        P(("head", "kv"), None),
        P(("head", "kv"), None),
        P(("head", "kv"), None),
        P(None, "kv", None),
        P(None, "kv", None),
        P(),
    )
    return jax.shard_map(
        shards, mesh=mesh, in_specs=placed, out_specs=P(("head", "kv"), None), check_vma=False
    )
```

```python
import math

import jax
import jax.numpy as jnp
import numpy as np
from jax import lax
from jax.experimental import pallas as pl
from jax.experimental.pallas import tpu as pltpu
from jax.sharding import PartitionSpec as P

HEADS = 32
KVH = 8
HD = 128
GROUP = HEADS // KVH
THETA = 500000.0
MESH = pl.DeviceIdType.MESH

NX, NY, NZ, NC = 4, 8, 8, 2
NG = NX * NC
NS = NZ * NC
OWN = KVH // NC
TOK = 4
ROWS = TOK * GROUP
ALL = NS * ROWS
FRESH = NY * NG * TOK
EXP_SCALE = HD ** (-0.5) * math.log2(math.e)
ORDER = (0, 1, 7, 2, 6, 3, 5, 4)
PLACE = tuple(ORDER.index(i) for i in range(8))
PIECES = 2
BLOCKS = 4
PART = NY // PIECES
PAIR = 2


def frequencies():
    half = HD // 2
    base = THETA ** (-(np.arange(half, dtype=np.float64) * 2.0 / HD))
    wave = 2.0 * np.pi / base
    smooth = (8192.0 / wave - 1.0) / 3.0
    blended = (1.0 - smooth) * base / 8.0 + smooth * base
    freq = np.where(wave < 2048.0, base, np.where(wave > 8192.0, base / 8.0, blended))
    return np.concatenate([freq, freq]).astype(np.float32)[None, :]


def kernel(
    start_hbm, freq_hbm, q_hbm, k_hbm, v_hbm, ck_ref, cv_ref, o_ref,
    start_ref, freq_ref, q_ref, k_ref, v_ref,
    sq, qall, ybuf, piece, kvb, acc, low, tot, so, ss, ro, rs, out,
    isem, csem, qsend, qrecv, ysend, yrecv, xsend, xrecv, osend, orecv, ssend, srecv,
):
    cached = ck_ref.shape[1]
    old = 2 * cached
    head, kv = lax.axis_index("head"), lax.axis_index("kv")
    x, y = lax.div(head, NY), lax.rem(head, NY)
    z, c = lax.div(kv, NC), lax.rem(kv, NC)
    g = x * NC + c
    mine, theirs = c * OWN, (1 - c) * OWN

    def of_row(other):
        return (lax.div(other, NC) * NY + y, z * NC + lax.rem(other, NC))

    column = [lax.rem(z + d, NZ) * NC + n for d in ORDER[1:] for n in range(NC)]
    partner = z * NC + (1 - c)
    column = [partner] + column
    ring = [lax.rem(y + d, NY) for d in ORDER[1:]]
    row = [lax.rem(g + i, NG) for i in range(1, NG)]
    back = column[::-1]

    barrier = pltpu.get_barrier_semaphore()
    peers = (
        [(head, i) for i in column] + [(x * NY + i, kv) for i in ring] + [of_row(i) for i in row]
    )
    for device in peers:
        pl.semaphore_signal(barrier, inc=1, device_id=device, device_id_type=MESH)

    inputs = [
        pltpu.make_async_copy(source, target, isem.at[i])
        for i, (source, target) in enumerate(
            (
                (start_hbm, start_ref), (freq_hbm, freq_ref), (q_hbm, q_ref), (k_hbm, k_ref),
                (v_hbm, v_ref),
            )
        )
    ]
    for copy in inputs:
        copy.start()
    caches = []
    for i, source in enumerate((ck_ref, cv_ref)):
        copy = pltpu.make_async_copy(
            source.at[pl.ds(mine, OWN)], kvb.at[i, :, pl.ds(0, cached)], csem.at[i]
        )
        copy.start()
        caches.append(copy)
    for copy in inputs:
        copy.wait()

    first = start_ref[0] + (head * NS + kv) * TOK
    places = first + lax.broadcasted_iota(jnp.int32, (TOK, HD), 0)
    angle = places.astype(jnp.float32) * freq_ref[...]
    lane = lax.broadcasted_iota(jnp.int32, (TOK, HD), 1)
    cosine = jnp.cos(angle)
    sine = jnp.sin(angle)
    sine = jnp.where(lane < HD // 2, -sine, sine)
    cos_q = jnp.concatenate([cosine] * GROUP, 0)
    sin_q = jnp.concatenate([sine] * GROUP, 0)
    for i in range(KVH):
        part = jnp.concatenate(
            [
                q_ref[:, (i * GROUP + j) * HD : (i * GROUP + j + 1) * HD].astype(jnp.float32)
                for j in range(GROUP)
            ],
            0,
        )
        turned = part * cos_q + pltpu.roll(part, HD // 2, 1) * sin_q
        sq[i] = turned.astype(jnp.bfloat16)
        part = k_ref[:, i * HD : (i + 1) * HD].astype(jnp.float32)
        turned = part * cosine + pltpu.roll(part, HD // 2, 1) * sine
        value = v_ref[:, i * HD : (i + 1) * HD].astype(jnp.float32)
        ybuf[0, i // OWN, i % OWN // PAIR, i % PAIR] = jnp.concatenate([turned, value], 0).astype(jnp.bfloat16)

    pl.semaphore_wait(barrier, len(peers))

    sends = []

    def send(source, target, sent, got, device):
        copy = pltpu.make_async_remote_copy(
            src_ref=source, dst_ref=target, send_sem=sent, recv_sem=got,
            device_id=device, device_id_type=MESH,
        )
        copy.start()
        sends.append(copy)

    def landed(target, got):
        pltpu.make_async_copy(target, target, got).wait()

    def spread(h):
        for i in column:
            half = sq.at[pl.ds(lax.rem(i, NC) * OWN + h * PAIR, PAIR)]
            target = qall.at[pl.ds(h * PAIR, PAIR), kv]
            send(half, target, qsend.at[h, i], qrecv.at[h, kv], (head, i))

    def along(h):
        for d, i in zip(ORDER[1:], ring):
            place = PLACE[(NY - d) % NY]
            send(
                ybuf.at[0, :, h], ybuf.at[place, :, h], ysend.at[h, place], yrecv.at[h, place],
                (x * NY + i, kv),
            )

    along(0)
    spread(0)
    along(1)
    spread(1)
    for i, source in enumerate((ck_ref, cv_ref)):
        send(
            source.at[pl.ds(theirs, OWN)], kvb.at[i, :, pl.ds(cached, cached)],
            csem.at[2 + i], csem.at[4 + i], (head, partner),
        )
    for j in range(OWN):
        qall[j, kv] = sq[mine + j]

    size = PART * TOK

    def gather(m, h):
        for i in range(m * PART, (m + 1) * PART):
            if i > 0:
                landed(ybuf.at[i, :, h], yrecv.at[h, i])
        for k in range(NC * PAIR):
            n, j = k // PAIR, k % PAIR
            four = [ybuf[m * PART + p, n, h, j].astype(jnp.float32) for p in range(PART)]
            j += n * OWN + h * PAIR
            at = slice(m * size, (m + 1) * size)
            piece[0, j, at] = jnp.concatenate([one[:TOK] for one in four], 0).astype(jnp.bfloat16)
            piece[1, j, at] = jnp.concatenate([one[TOK:] for one in four], 0).astype(jnp.bfloat16)

    def rows_of(i, m, count=1):
        return pl.ds(pl.multiple_of(old + (i * PIECES + m) * size, size), count * size)

    def forward(h, m, count):
        two = pl.ds(h * PAIR, PAIR)
        at = pl.ds(m * size, count * size)
        for i in row:
            half = piece.at[:, pl.ds(lax.rem(i, NC) * OWN + h * PAIR, PAIR), at]
            target = kvb.at[:, two, rows_of(g, m, count)]
            send(half, target, xsend.at[h, m, i], xrecv.at[h, m, g], of_row(i))
        for j in range(h * PAIR, (h + 1) * PAIR):
            for n in range(2):
                kvb[n, j, rows_of(g, m, count)] = piece[n, mine + j, m * size : (m + count) * size]

    gather(0, 0)
    forward(0, 0, 1)
    gather(1, 0)
    forward(0, 1, 1)
    gather(0, 1)
    gather(1, 1)
    forward(1, 0, PIECES)

    for i, copy in enumerate(caches):
        copy.wait()
        landed(kvb.at[i, :, pl.ds(cached, cached)], csem.at[4 + i])

    def scores_of(j, keys):
        return lax.dot_general(
            qall[j].reshape(ALL, HD), keys, (((1,), (1,)), ((), ())),
            preferred_element_type=jnp.float32,
        )

    def weigh(probs, values):
        ones = jnp.ones(values.shape, jnp.bfloat16)
        both = jnp.dot(
            probs, jnp.concatenate([values, ones], 1), preferred_element_type=jnp.float32
        )
        return both[:, :HD], both[:, HD:]

    def on_cached(j, carry):
        block = old // BLOCKS
        top = output = total = None
        for n in range(BLOCKS):
            keys = slice(n * block, (n + 1) * block)
            scores = scores_of(j, kvb[0, j, keys])
            here = jnp.broadcast_to(jnp.max(scores, 1, keepdims=True) * EXP_SCALE, (ALL, HD))
            peak = here if n == 0 else jnp.maximum(top, here)
            wide = jnp.concatenate([peak] * (block // HD), 1)
            probs = jnp.exp2(scores * EXP_SCALE - wide).astype(jnp.bfloat16)
            added, summed = weigh(probs, kvb[1, j, keys])
            if n == 0:
                output, total = added, summed
            else:
                keep = jnp.exp2(top - peak)
                output = output * keep + added
                total = total * keep + summed
            top = peak
        acc[j] = output
        tot[j] = total
        low[j] = top
        return carry

    at_row = lax.broadcasted_iota(jnp.int32, (ALL, FRESH), 0)
    at_key = lax.broadcasted_iota(jnp.int32, (ALL, FRESH), 1)
    row_token = (head * NS + lax.div(at_row, ROWS)) * TOK + lax.rem(at_row, TOK)
    source = lax.div(at_key, NY * TOK)
    place = lax.rem(lax.div(at_key, TOK), NY)
    away = lax.div(place + 1, 2)
    away = jnp.where(lax.rem(place, 2) == 1, away, NY - away)
    key_head = lax.div(source, NC) * NY + lax.rem(y + away, NY)
    key_token = (key_head * NS + z * NC + lax.rem(source, NC)) * TOK + lax.rem(at_key, TOK)
    visible = key_token <= row_token
    lane_row = lax.broadcasted_iota(jnp.int32, (ALL, HD), 1) - lax.rem(
        lax.broadcasted_iota(jnp.int32, (ALL, HD), 0), ROWS
    )

    ss[...] = jnp.zeros_like(ss)
    for h in range(OWN // PAIR):
        two = pl.ds(h * PAIR, PAIR)
        for i in column:
            landed(qall.at[two, i], qrecv.at[h, i])
        lax.fori_loop(h * PAIR, (h + 1) * PAIR, on_cached, 0, unroll=True)
        for m in range(PIECES if h == 0 else 1):
            for i in row:
                landed(kvb.at[:, two, rows_of(i, m, h + 1)], xrecv.at[h, m, i])
        for j in range(h * PAIR, (h + 1) * PAIR):
            scores = jnp.where(visible, scores_of(j, kvb[0, j, old:]), -1e30)
            before = low[j]
            top = jnp.maximum(before, jnp.max(scores, 1, keepdims=True) * EXP_SCALE)
            both = jnp.concatenate([top] * (FRESH // HD), 1)
            probs = jnp.exp2(scores * EXP_SCALE - both).astype(jnp.bfloat16)
            output, total = weigh(probs, kvb[1, j, old:])
            keep = jnp.exp2(before - top)
            output = acc[j] * keep + output
            total = tot[j] * keep + total
            level = top + jnp.log2(total)
            output = (output / total).astype(jnp.bfloat16)
            so[:, j] = output.reshape(NS, ROWS, HD)
            level = jnp.where(lane_row == j * ROWS, level, 0.0).reshape(NS, ROWS, HD)
            ss[...] += jnp.sum(level, 1, keepdims=True)
        for i in back:
            send(so.at[i, two], ro.at[kv, two], osend.at[h, i], orecv.at[h, kv], (head, i))
            if h == OWN // PAIR - 1:
                send(ss.at[i], rs.at[kv], ssend.at[i], srecv.at[kv], (head, i))
    ro[kv] = so[kv]
    rs[kv] = ss[kv]

    for i in column:
        landed(rs.at[i], srecv.at[i])
    levels = rs[:, 0, :].reshape(NZ, NC, HD)
    weight = jnp.exp2(levels - jnp.max(levels, 0, keepdims=True))
    weight = weight / jnp.sum(weight, 0, keepdims=True)
    weight = jnp.transpose(weight.reshape(NS, HD))
    for i in column:
        for m in range(OWN // PAIR):
            two = pl.ds(m * PAIR, PAIR)
            landed(ro.at[i, two], orecv.at[m, i])
    for n in range(NC):
        for j in range(OWN):
            total = jnp.zeros((ROWS, HD), jnp.float32)
            for i in range(NZ):
                at = i * NC + n
                share = weight[j * ROWS : (j + 1) * ROWS, at : at + 1]
                total = total + share * ro[at, j].astype(jnp.float32)
            for h in range(GROUP):
                at = ((n * OWN + j) * GROUP + h) * HD
                out[:, at : at + HD] = total[h * TOK : (h + 1) * TOK].astype(jnp.bfloat16)
    done = pltpu.make_async_copy(out, o_ref, isem.at[0])
    done.start()
    for copy in sends:
        copy.wait_send()
    done.wait()


def shards(queries, new_keys, new_values, cache_keys, cache_values, start):
    keys = 2 * cache_keys.shape[1] + FRESH
    hbm = pl.BlockSpec(memory_space=pltpu.HBM)
    dma = pltpu.SemaphoreType.DMA
    bf16 = jnp.bfloat16
    f32 = jnp.float32
    return pl.pallas_call(
        kernel,
        out_shape=jax.ShapeDtypeStruct((TOK, HEADS * HD), bf16),
        in_specs=[hbm] * 7,
        out_specs=pl.BlockSpec(memory_space=pl.ANY),
        scratch_shapes=[
            pltpu.SMEM((1,), jnp.int32),
            pltpu.VMEM((1, HD), f32),
            pltpu.VMEM((TOK, HEADS * HD), bf16),
            pltpu.VMEM((TOK, KVH * HD), bf16),
            pltpu.VMEM((TOK, KVH * HD), bf16),
            pltpu.VMEM((KVH, ROWS, HD), bf16),
            pltpu.VMEM((OWN, NS, ROWS, HD), bf16),
            pltpu.VMEM((NY, NC, OWN // PAIR, PAIR, 2 * TOK, HD), bf16),
            pltpu.VMEM((2, KVH, PIECES * PART * TOK, HD), bf16),
            pltpu.VMEM((2, OWN, keys, HD), bf16),
            pltpu.VMEM((OWN, ALL, HD), f32),
            pltpu.VMEM((OWN, ALL, HD), f32),
            pltpu.VMEM((OWN, ALL, HD), f32),
            pltpu.VMEM((NS, OWN, ROWS, HD), bf16),
            pltpu.VMEM((NS, 1, HD), f32),
            pltpu.VMEM((NS, OWN, ROWS, HD), bf16),
            pltpu.VMEM((NS, 1, HD), f32),
            pltpu.VMEM((TOK, HEADS * HD), bf16),
            dma((5,)), dma((6,)), dma((2, NS)), dma((2, NS)), dma((2, NY)), dma((2, NY)),
            dma((2, PIECES, NG)), dma((2, PIECES, NG)), dma((2, NS)), dma((2, NS)), dma((NS,)), dma((NS,)),
        ],
        compiler_params=pltpu.CompilerParams(
            collective_id=0, has_side_effects=True, vmem_limit_bytes=40000 * 1024
        ),
    )(
        start,
        *[
            pltpu.with_memory_space_constraint(one, pltpu.HBM)
            for one in (
                jnp.asarray(frequencies()), queries, new_keys, new_values, cache_keys, cache_values
            )
        ],
    )


def solution(mesh):
    placed = (
        P(("head", "kv"), None),
        P(("head", "kv"), None),
        P(("head", "kv"), None),
        P(None, "kv", None),
        P(None, "kv", None),
        P(),
    )
    return jax.shard_map(
        shards, mesh=mesh, in_specs=placed, out_specs=P(("head", "kv"), None), check_vma=False
    )
```

```python
import math

import jax
import jax.numpy as jnp
import numpy as np
from jax import lax
from jax.experimental import pallas as pl
from jax.experimental.pallas import tpu as pltpu
from jax.sharding import PartitionSpec as P

HEADS = 32
KVH = 8
HD = 128
GROUP = HEADS // KVH
THETA = 500000.0
MESH = pl.DeviceIdType.MESH

NX, NY, NZ, NC = 4, 8, 8, 2
NG = NX * NC
NS = NZ * NC
OWN = KVH // NC
TOK = 4
ROWS = TOK * GROUP
ALL = NS * ROWS
FRESH = NY * NG * TOK
EXP_SCALE = HD ** (-0.5) * math.log2(math.e)
ORDER = (0, 1, 7, 2, 6, 3, 5, 4)
PLACE = tuple(ORDER.index(i) for i in range(8))
PIECES = 2
BLOCKS = 4
PART = NY // PIECES
PAIR = 2


def frequencies():
    half = HD // 2
    base = THETA ** (-(np.arange(half, dtype=np.float64) * 2.0 / HD))
    wave = 2.0 * np.pi / base
    smooth = (8192.0 / wave - 1.0) / 3.0
    blended = (1.0 - smooth) * base / 8.0 + smooth * base
    freq = np.where(wave < 2048.0, base, np.where(wave > 8192.0, base / 8.0, blended))
    return np.concatenate([freq, freq]).astype(np.float32)[None, :]


def kernel(
    start_hbm, freq_hbm, q_hbm, k_hbm, v_hbm, ck_ref, cv_ref, o_ref,
    start_ref, freq_ref, q_ref, k_ref, v_ref,
    sq, qall, ybuf, piece, kvb, acc, low, tot, so, ss, ro, rs, out,
    isem, csem, qsend, qrecv, ysend, yrecv, xsend, xrecv, osend, orecv, ssend, srecv,
):
    cached = ck_ref.shape[1]
    old = 2 * cached
    head, kv = lax.axis_index("head"), lax.axis_index("kv")
    x, y = lax.div(head, NY), lax.rem(head, NY)
    z, c = lax.div(kv, NC), lax.rem(kv, NC)
    g = x * NC + c
    mine, theirs = c * OWN, (1 - c) * OWN

    def of_row(other):
        return (lax.div(other, NC) * NY + y, z * NC + lax.rem(other, NC))

    column = [lax.rem(z + d, NZ) * NC + n for d in ORDER[1:] for n in range(NC)]
    partner = z * NC + (1 - c)
    column = [partner] + column
    ring = [lax.rem(y + d, NY) for d in ORDER[1:]]
    row = [lax.rem(g + i, NG) for i in range(1, NG)]
    back = column[::-1]

    barrier = pltpu.get_barrier_semaphore()
    peers = (
        [(head, i) for i in column] + [(x * NY + i, kv) for i in ring] + [of_row(i) for i in row]
    )
    for device in peers[::-1]:
        pl.semaphore_signal(barrier, inc=1, device_id=device, device_id_type=MESH)

    inputs = [
        pltpu.make_async_copy(source, target, isem.at[i])
        for i, (source, target) in enumerate(
            (
                (start_hbm, start_ref), (freq_hbm, freq_ref), (q_hbm, q_ref), (k_hbm, k_ref),
                (v_hbm, v_ref),
            )
        )
    ]
    for copy in inputs:
        copy.start()
    caches = []
    for i, source in enumerate((ck_ref, cv_ref)):
        copy = pltpu.make_async_copy(
            source.at[pl.ds(mine, OWN)], kvb.at[i, :, pl.ds(0, cached)], csem.at[i]
        )
        copy.start()
        caches.append(copy)
    for copy in inputs:
        copy.wait()

    first = start_ref[0] + (head * NS + kv) * TOK
    places = first + lax.broadcasted_iota(jnp.int32, (TOK, HD), 0)
    angle = places.astype(jnp.float32) * freq_ref[...]
    lane = lax.broadcasted_iota(jnp.int32, (TOK, HD), 1)
    cosine = jnp.cos(angle)
    sine = jnp.sin(angle)
    sine = jnp.where(lane < HD // 2, -sine, sine)
    cos_q = jnp.concatenate([cosine] * GROUP, 0)
    sin_q = jnp.concatenate([sine] * GROUP, 0)
    for i in range(KVH):
        part = jnp.concatenate(
            [
                q_ref[:, (i * GROUP + j) * HD : (i * GROUP + j + 1) * HD].astype(jnp.float32)
                for j in range(GROUP)
            ],
            0,
        )
        turned = part * cos_q + pltpu.roll(part, HD // 2, 1) * sin_q
        sq[i] = turned.astype(jnp.bfloat16)
        part = k_ref[:, i * HD : (i + 1) * HD].astype(jnp.float32)
        turned = part * cosine + pltpu.roll(part, HD // 2, 1) * sine
        value = v_ref[:, i * HD : (i + 1) * HD].astype(jnp.float32)
        ybuf[0, i // OWN, i % OWN // PAIR, i % PAIR] = jnp.concatenate([turned, value], 0).astype(jnp.bfloat16)

    pl.semaphore_wait(barrier, len(peers))

    sends = []

    def send(source, target, sent, got, device):
        copy = pltpu.make_async_remote_copy(
            src_ref=source, dst_ref=target, send_sem=sent, recv_sem=got,
            device_id=device, device_id_type=MESH,
        )
        copy.start()
        sends.append(copy)

    def landed(target, got):
        pltpu.make_async_copy(target, target, got).wait()

    def spread(h):
        for i in column:
            half = sq.at[pl.ds(lax.rem(i, NC) * OWN + h * PAIR, PAIR)]
            target = qall.at[pl.ds(h * PAIR, PAIR), kv]
            send(half, target, qsend.at[h, i], qrecv.at[h, kv], (head, i))

    def along(h):
        for d, i in zip(ORDER[1:], ring):
            place = PLACE[(NY - d) % NY]
            send(
                ybuf.at[0, :, h], ybuf.at[place, :, h], ysend.at[h, place], yrecv.at[h, place],
                (x * NY + i, kv),
            )

    along(0)
    spread(0)
    for i, source in enumerate((ck_ref, cv_ref)):
        send(
            source.at[pl.ds(theirs, OWN)], kvb.at[i, :, pl.ds(cached, cached)],
            csem.at[2 + i], csem.at[4 + i], (head, partner),
        )
    along(1)
    spread(1)
    for j in range(OWN):
        qall[j, kv] = sq[mine + j]

    size = PART * TOK

    def gather(m, h):
        for i in range(m * PART, (m + 1) * PART):
            if i > 0:
                landed(ybuf.at[i, :, h], yrecv.at[h, i])
        for k in range(NC * PAIR):
            n, j = k // PAIR, k % PAIR
            four = [ybuf[m * PART + p, n, h, j].astype(jnp.float32) for p in range(PART)]
            j += n * OWN + h * PAIR
            at = slice(m * size, (m + 1) * size)
            piece[0, j, at] = jnp.concatenate([one[:TOK] for one in four], 0).astype(jnp.bfloat16)
            piece[1, j, at] = jnp.concatenate([one[TOK:] for one in four], 0).astype(jnp.bfloat16)

    def rows_of(i, m, count=1):
        return pl.ds(pl.multiple_of(old + (i * PIECES + m) * size, size), count * size)

    def forward(h, m, count):
        two = pl.ds(h * PAIR, PAIR)
        at = pl.ds(m * size, count * size)
        for i in row:
            half = piece.at[:, pl.ds(lax.rem(i, NC) * OWN + h * PAIR, PAIR), at]
            target = kvb.at[:, two, rows_of(g, m, count)]
            send(half, target, xsend.at[h, m, i], xrecv.at[h, m, g], of_row(i))
        for j in range(h * PAIR, (h + 1) * PAIR):
            for n in range(2):
                kvb[n, j, rows_of(g, m, count)] = piece[n, mine + j, m * size : (m + count) * size]

    gather(0, 0)
    forward(0, 0, 1)
    gather(1, 0)
    forward(0, 1, 1)
    gather(0, 1)
    gather(1, 1)
    forward(1, 0, PIECES)

    for i, copy in enumerate(caches):
        copy.wait()
        landed(kvb.at[i, :, pl.ds(cached, cached)], csem.at[4 + i])

    def scores_of(j, keys):
        return lax.dot_general(
            qall[j].reshape(ALL, HD), keys, (((1,), (1,)), ((), ())),
            preferred_element_type=jnp.float32,
        )

    def weigh(probs, values):
        ones = jnp.ones(values.shape, jnp.bfloat16)
        both = jnp.dot(
            probs, jnp.concatenate([values, ones], 1), preferred_element_type=jnp.float32
        )
        return both[:, :HD], both[:, HD:]

    def on_cached(j, carry):
        block = old // BLOCKS
        top = output = total = None
        for n in range(BLOCKS):
            keys = slice(n * block, (n + 1) * block)
            scores = scores_of(j, kvb[0, j, keys])
            here = jnp.broadcast_to(jnp.max(scores, 1, keepdims=True) * EXP_SCALE, (ALL, HD))
            peak = here if n == 0 else jnp.maximum(top, here)
            wide = jnp.concatenate([peak] * (block // HD), 1)
            probs = jnp.exp2(scores * EXP_SCALE - wide).astype(jnp.bfloat16)
            added, summed = weigh(probs, kvb[1, j, keys])
            if n == 0:
                output, total = added, summed
            else:
                keep = jnp.exp2(top - peak)
                output = output * keep + added
                total = total * keep + summed
            top = peak
        acc[j] = output
        tot[j] = total
        low[j] = top
        return carry

    at_row = lax.broadcasted_iota(jnp.int32, (ALL, FRESH), 0)
    at_key = lax.broadcasted_iota(jnp.int32, (ALL, FRESH), 1)
    row_token = (head * NS + lax.div(at_row, ROWS)) * TOK + lax.rem(at_row, TOK)
    source = lax.div(at_key, NY * TOK)
    place = lax.rem(lax.div(at_key, TOK), NY)
    away = lax.div(place + 1, 2)
    away = jnp.where(lax.rem(place, 2) == 1, away, NY - away)
    key_head = lax.div(source, NC) * NY + lax.rem(y + away, NY)
    key_token = (key_head * NS + z * NC + lax.rem(source, NC)) * TOK + lax.rem(at_key, TOK)
    visible = key_token <= row_token
    lane_row = lax.broadcasted_iota(jnp.int32, (ALL, HD), 1) - lax.rem(
        lax.broadcasted_iota(jnp.int32, (ALL, HD), 0), ROWS
    )

    ss[...] = jnp.zeros_like(ss)
    for h in range(OWN // PAIR):
        two = pl.ds(h * PAIR, PAIR)
        for i in column:
            landed(qall.at[two, i], qrecv.at[h, i])
        lax.fori_loop(h * PAIR, (h + 1) * PAIR, on_cached, 0, unroll=True)
        for m in range(PIECES if h == 0 else 1):
            for i in row:
                landed(kvb.at[:, two, rows_of(i, m, h + 1)], xrecv.at[h, m, i])
        for j in range(h * PAIR, (h + 1) * PAIR):
            scores = jnp.where(visible, scores_of(j, kvb[0, j, old:]), -1e30)
            before = low[j]
            top = jnp.maximum(before, jnp.max(scores, 1, keepdims=True) * EXP_SCALE)
            both = jnp.concatenate([top] * (FRESH // HD), 1)
            probs = jnp.exp2(scores * EXP_SCALE - both).astype(jnp.bfloat16)
            output, total = weigh(probs, kvb[1, j, old:])
            keep = jnp.exp2(before - top)
            output = acc[j] * keep + output
            total = tot[j] * keep + total
            level = top + jnp.log2(total)
            output = (output / total).astype(jnp.bfloat16)
            so[:, j] = output.reshape(NS, ROWS, HD)
            level = jnp.where(lane_row == j * ROWS, level, 0.0).reshape(NS, ROWS, HD)
            ss[...] += jnp.sum(level, 1, keepdims=True)
        for i in back:
            send(so.at[i, two], ro.at[kv, two], osend.at[h, i], orecv.at[h, kv], (head, i))
            if h == OWN // PAIR - 1:
                send(ss.at[i], rs.at[kv], ssend.at[i], srecv.at[kv], (head, i))
    ro[kv] = so[kv]
    rs[kv] = ss[kv]

    for i in column:
        landed(rs.at[i], srecv.at[i])
    levels = rs[:, 0, :].reshape(NZ, NC, HD)
    weight = jnp.exp2(levels - jnp.max(levels, 0, keepdims=True))
    weight = weight / jnp.sum(weight, 0, keepdims=True)
    weight = jnp.transpose(weight.reshape(NS, HD))
    for i in column:
        for m in range(OWN // PAIR):
            two = pl.ds(m * PAIR, PAIR)
            landed(ro.at[i, two], orecv.at[m, i])
    for n in range(NC):
        for j in range(OWN):
            total = jnp.zeros((ROWS, HD), jnp.float32)
            for i in range(NZ):
                at = i * NC + n
                share = weight[j * ROWS : (j + 1) * ROWS, at : at + 1]
                total = total + share * ro[at, j].astype(jnp.float32)
            for h in range(GROUP):
                at = ((n * OWN + j) * GROUP + h) * HD
                out[:, at : at + HD] = total[h * TOK : (h + 1) * TOK].astype(jnp.bfloat16)
    done = pltpu.make_async_copy(out, o_ref, isem.at[0])
    done.start()
    for copy in sends:
        copy.wait_send()
    done.wait()


def shards(queries, new_keys, new_values, cache_keys, cache_values, start):
    keys = 2 * cache_keys.shape[1] + FRESH
    hbm = pl.BlockSpec(memory_space=pltpu.HBM)
    dma = pltpu.SemaphoreType.DMA
    bf16 = jnp.bfloat16
    f32 = jnp.float32
    return pl.pallas_call(
        kernel,
        out_shape=jax.ShapeDtypeStruct((TOK, HEADS * HD), bf16),
        in_specs=[hbm] * 7,
        out_specs=pl.BlockSpec(memory_space=pl.ANY),
        scratch_shapes=[
            pltpu.SMEM((1,), jnp.int32),
            pltpu.VMEM((1, HD), f32),
            pltpu.VMEM((TOK, HEADS * HD), bf16),
            pltpu.VMEM((TOK, KVH * HD), bf16),
            pltpu.VMEM((TOK, KVH * HD), bf16),
            pltpu.VMEM((KVH, ROWS, HD), bf16),
            pltpu.VMEM((OWN, NS, ROWS, HD), bf16),
            pltpu.VMEM((NY, NC, OWN // PAIR, PAIR, 2 * TOK, HD), bf16),
            pltpu.VMEM((2, KVH, PIECES * PART * TOK, HD), bf16),
            pltpu.VMEM((2, OWN, keys, HD), bf16),
            pltpu.VMEM((OWN, ALL, HD), f32),
            pltpu.VMEM((OWN, ALL, HD), f32),
            pltpu.VMEM((OWN, ALL, HD), f32),
            pltpu.VMEM((NS, OWN, ROWS, HD), bf16),
            pltpu.VMEM((NS, 1, HD), f32),
            pltpu.VMEM((NS, OWN, ROWS, HD), bf16),
            pltpu.VMEM((NS, 1, HD), f32),
            pltpu.VMEM((TOK, HEADS * HD), bf16),
            dma((5,)), dma((6,)), dma((2, NS)), dma((2, NS)), dma((2, NY)), dma((2, NY)),
            dma((2, PIECES, NG)), dma((2, PIECES, NG)), dma((2, NS)), dma((2, NS)), dma((NS,)), dma((NS,)),
        ],
        compiler_params=pltpu.CompilerParams(
            collective_id=0, has_side_effects=True, vmem_limit_bytes=40000 * 1024
        ),
    )(
        start,
        *[
            pltpu.with_memory_space_constraint(one, pltpu.HBM)
            for one in (
                jnp.asarray(frequencies()), queries, new_keys, new_values, cache_keys, cache_values
            )
        ],
    )


def solution(mesh):
    placed = (
        P(("head", "kv"), None),
        P(("head", "kv"), None),
        P(("head", "kv"), None),
        P(None, "kv", None),
        P(None, "kv", None),
        P(),
    )
    return jax.shard_map(
        shards, mesh=mesh, in_specs=placed, out_specs=P(("head", "kv"), None), check_vma=False
    )
```

```python
import math

import jax
import jax.numpy as jnp
import numpy as np
from jax import lax
from jax.experimental import pallas as pl
from jax.experimental.pallas import tpu as pltpu
from jax.sharding import PartitionSpec as P

HEADS = 32
KVH = 8
HD = 128
GROUP = HEADS // KVH
THETA = 500000.0
MESH = pl.DeviceIdType.MESH

NX, NY, NZ, NC = 4, 8, 8, 2
NG = NX * NC
NS = NZ * NC
OWN = KVH // NC
TOK = 4
ROWS = TOK * GROUP
ALL = NS * ROWS
FRESH = NY * NG * TOK
EXP_SCALE = HD ** (-0.5) * math.log2(math.e)
ORDER = (0, 1, 7, 2, 6, 3, 5, 4)
PLACE = tuple(ORDER.index(i) for i in range(8))
PIECES = 2
BLOCKS = 8
PART = NY // PIECES
PAIR = 2


def frequencies():
    half = HD // 2
    base = THETA ** (-(np.arange(half, dtype=np.float64) * 2.0 / HD))
    wave = 2.0 * np.pi / base
    smooth = (8192.0 / wave - 1.0) / 3.0
    blended = (1.0 - smooth) * base / 8.0 + smooth * base
    freq = np.where(wave < 2048.0, base, np.where(wave > 8192.0, base / 8.0, blended))
    return np.concatenate([freq, freq]).astype(np.float32)[None, :]


def kernel(
    start_hbm, freq_hbm, q_hbm, k_hbm, v_hbm, ck_ref, cv_ref, o_ref,
    start_ref, freq_ref, q_ref, k_ref, v_ref,
    sq, qall, ybuf, piece, kvb, acc, low, tot, so, ss, ro, rs, out,
    isem, csem, qsend, qrecv, ysend, yrecv, xsend, xrecv, osend, orecv, ssend, srecv,
):
    cached = ck_ref.shape[1]
    old = 2 * cached
    head, kv = lax.axis_index("head"), lax.axis_index("kv")
    x, y = lax.div(head, NY), lax.rem(head, NY)
    z, c = lax.div(kv, NC), lax.rem(kv, NC)
    g = x * NC + c
    mine, theirs = c * OWN, (1 - c) * OWN

    def of_row(other):
        return (lax.div(other, NC) * NY + y, z * NC + lax.rem(other, NC))

    column = [lax.rem(z + d, NZ) * NC + n for d in ORDER[1:] for n in range(NC)]
    partner = z * NC + (1 - c)
    column = [partner] + column
    ring = [lax.rem(y + d, NY) for d in ORDER[1:]]
    row = [lax.rem(g + i, NG) for i in range(1, NG)]
    back = column[::-1]

    barrier = pltpu.get_barrier_semaphore()
    peers = (
        [(head, i) for i in column] + [(x * NY + i, kv) for i in ring] + [of_row(i) for i in row]
    )
    for device in peers[::-1]:
        pl.semaphore_signal(barrier, inc=1, device_id=device, device_id_type=MESH)

    inputs = [
        pltpu.make_async_copy(source, target, isem.at[i])
        for i, (source, target) in enumerate(
            (
                (start_hbm, start_ref), (freq_hbm, freq_ref), (q_hbm, q_ref), (k_hbm, k_ref),
                (v_hbm, v_ref),
            )
        )
    ]
    for copy in inputs:
        copy.start()
    caches = []
    for i, source in enumerate((ck_ref, cv_ref)):
        copy = pltpu.make_async_copy(
            source.at[pl.ds(mine, OWN)], kvb.at[i, :, pl.ds(0, cached)], csem.at[i]
        )
        copy.start()
        caches.append(copy)
    for copy in inputs:
        copy.wait()

    first = start_ref[0] + (head * NS + kv) * TOK
    places = first + lax.broadcasted_iota(jnp.int32, (TOK, HD), 0)
    angle = places.astype(jnp.float32) * freq_ref[...]
    lane = lax.broadcasted_iota(jnp.int32, (TOK, HD), 1)
    cosine = jnp.cos(angle)
    sine = jnp.sin(angle)
    sine = jnp.where(lane < HD // 2, -sine, sine)
    cos_q = jnp.concatenate([cosine] * GROUP, 0)
    sin_q = jnp.concatenate([sine] * GROUP, 0)
    for i in range(KVH):
        part = jnp.concatenate(
            [
                q_ref[:, (i * GROUP + j) * HD : (i * GROUP + j + 1) * HD].astype(jnp.float32)
                for j in range(GROUP)
            ],
            0,
        )
        turned = part * cos_q + pltpu.roll(part, HD // 2, 1) * sin_q
        sq[i] = turned.astype(jnp.bfloat16)
        part = k_ref[:, i * HD : (i + 1) * HD].astype(jnp.float32)
        turned = part * cosine + pltpu.roll(part, HD // 2, 1) * sine
        value = v_ref[:, i * HD : (i + 1) * HD].astype(jnp.float32)
        ybuf[0, i // OWN, i % OWN // PAIR, i % PAIR] = jnp.concatenate([turned, value], 0).astype(jnp.bfloat16)

    pl.semaphore_wait(barrier, len(peers))

    sends = []

    def send(source, target, sent, got, device):
        copy = pltpu.make_async_remote_copy(
            src_ref=source, dst_ref=target, send_sem=sent, recv_sem=got,
            device_id=device, device_id_type=MESH,
        )
        copy.start()
        sends.append(copy)

    def landed(target, got):
        pltpu.make_async_copy(target, target, got).wait()

    def spread(h):
        for i in column:
            half = sq.at[pl.ds(lax.rem(i, NC) * OWN + h * PAIR, PAIR)]
            target = qall.at[pl.ds(h * PAIR, PAIR), kv]
            send(half, target, qsend.at[h, i], qrecv.at[h, kv], (head, i))

    def along(h):
        for d, i in zip(ORDER[1:], ring):
            place = PLACE[(NY - d) % NY]
            send(
                ybuf.at[0, :, h], ybuf.at[place, :, h], ysend.at[h, place], yrecv.at[h, place],
                (x * NY + i, kv),
            )

    along(0)
    spread(0)
    for i, source in enumerate((ck_ref, cv_ref)):
        send(
            source.at[pl.ds(theirs, OWN)], kvb.at[i, :, pl.ds(cached, cached)],
            csem.at[2 + i], csem.at[4 + i], (head, partner),
        )
    along(1)
    spread(1)
    for j in range(OWN):
        qall[j, kv] = sq[mine + j]

    size = PART * TOK

    def gather(m, h):
        for i in range(m * PART, (m + 1) * PART):
            if i > 0:
                landed(ybuf.at[i, :, h], yrecv.at[h, i])
        for k in range(NC * PAIR):
            n, j = k // PAIR, k % PAIR
            four = [ybuf[m * PART + p, n, h, j].astype(jnp.float32) for p in range(PART)]
            j += n * OWN + h * PAIR
            at = slice(m * size, (m + 1) * size)
            piece[0, j, at] = jnp.concatenate([one[:TOK] for one in four], 0).astype(jnp.bfloat16)
            piece[1, j, at] = jnp.concatenate([one[TOK:] for one in four], 0).astype(jnp.bfloat16)

    def rows_of(i, m, count=1):
        return pl.ds(pl.multiple_of(old + (i * PIECES + m) * size, size), count * size)

    def forward(h, m, count):
        two = pl.ds(h * PAIR, PAIR)
        at = pl.ds(m * size, count * size)
        for i in row:
            half = piece.at[:, pl.ds(lax.rem(i, NC) * OWN + h * PAIR, PAIR), at]
            target = kvb.at[:, two, rows_of(g, m, count)]
            send(half, target, xsend.at[h, m, i], xrecv.at[h, m, g], of_row(i))
        for j in range(h * PAIR, (h + 1) * PAIR):
            for n in range(2):
                kvb[n, j, rows_of(g, m, count)] = piece[n, mine + j, m * size : (m + count) * size]

    gather(0, 0)
    forward(0, 0, 1)
    gather(1, 0)
    forward(0, 1, 1)
    gather(0, 1)
    gather(1, 1)
    forward(1, 0, PIECES)

    for i, copy in enumerate(caches):
        copy.wait()
        landed(kvb.at[i, :, pl.ds(cached, cached)], csem.at[4 + i])

    def scores_of(j, keys):
        return lax.dot_general(
            qall[j].reshape(ALL, HD), keys, (((1,), (1,)), ((), ())),
            preferred_element_type=jnp.float32,
        )

    def weigh(probs, values):
        ones = jnp.ones(values.shape, jnp.bfloat16)
        both = jnp.dot(
            probs, jnp.concatenate([values, ones], 1), preferred_element_type=jnp.float32
        )
        return both[:, :HD], both[:, HD:]

    def on_cached(j, carry):
        block = old // BLOCKS
        top = output = total = None
        for n in range(BLOCKS):
            keys = slice(n * block, (n + 1) * block)
            scores = scores_of(j, kvb[0, j, keys])
            here = jnp.broadcast_to(jnp.max(scores, 1, keepdims=True) * EXP_SCALE, (ALL, HD))
            peak = here if n == 0 else jnp.maximum(top, here)
            wide = jnp.concatenate([peak] * (block // HD), 1)
            probs = jnp.exp2(scores * EXP_SCALE - wide).astype(jnp.bfloat16)
            added, summed = weigh(probs, kvb[1, j, keys])
            if n == 0:
                output, total = added, summed
            else:
                keep = jnp.exp2(top - peak)
                output = output * keep + added
                total = total * keep + summed
            top = peak
        acc[j] = output
        tot[j] = total
        low[j] = top
        return carry

    at_row = lax.broadcasted_iota(jnp.int32, (ALL, FRESH), 0)
    at_key = lax.broadcasted_iota(jnp.int32, (ALL, FRESH), 1)
    row_token = (head * NS + lax.div(at_row, ROWS)) * TOK + lax.rem(at_row, TOK)
    source = lax.div(at_key, NY * TOK)
    place = lax.rem(lax.div(at_key, TOK), NY)
    away = lax.div(place + 1, 2)
    away = jnp.where(lax.rem(place, 2) == 1, away, NY - away)
    key_head = lax.div(source, NC) * NY + lax.rem(y + away, NY)
    key_token = (key_head * NS + z * NC + lax.rem(source, NC)) * TOK + lax.rem(at_key, TOK)
    visible = key_token <= row_token
    lane_row = lax.broadcasted_iota(jnp.int32, (ALL, HD), 1) - lax.rem(
        lax.broadcasted_iota(jnp.int32, (ALL, HD), 0), ROWS
    )

    ss[...] = jnp.zeros_like(ss)
    for h in range(OWN // PAIR):
        two = pl.ds(h * PAIR, PAIR)
        for i in column:
            landed(qall.at[two, i], qrecv.at[h, i])
        lax.fori_loop(h * PAIR, (h + 1) * PAIR, on_cached, 0, unroll=True)
        for m in range(PIECES if h == 0 else 1):
            for i in row:
                landed(kvb.at[:, two, rows_of(i, m, h + 1)], xrecv.at[h, m, i])
        for j in range(h * PAIR, (h + 1) * PAIR):
            scores = jnp.where(visible, scores_of(j, kvb[0, j, old:]), -1e30)
            before = low[j]
            top = jnp.maximum(before, jnp.max(scores, 1, keepdims=True) * EXP_SCALE)
            both = jnp.concatenate([top] * (FRESH // HD), 1)
            probs = jnp.exp2(scores * EXP_SCALE - both).astype(jnp.bfloat16)
            output, total = weigh(probs, kvb[1, j, old:])
            keep = jnp.exp2(before - top)
            output = acc[j] * keep + output
            total = tot[j] * keep + total
            level = top + jnp.log2(total)
            output = (output / total).astype(jnp.bfloat16)
            so[:, j] = output.reshape(NS, ROWS, HD)
            level = jnp.where(lane_row == j * ROWS, level, 0.0).reshape(NS, ROWS, HD)
            ss[...] += jnp.sum(level, 1, keepdims=True)
        for i in back:
            send(so.at[i, two], ro.at[kv, two], osend.at[h, i], orecv.at[h, kv], (head, i))
            if h == OWN // PAIR - 1:
                send(ss.at[i], rs.at[kv], ssend.at[i], srecv.at[kv], (head, i))
    ro[kv] = so[kv]
    rs[kv] = ss[kv]

    for i in column:
        landed(rs.at[i], srecv.at[i])
    levels = rs[:, 0, :].reshape(NZ, NC, HD)
    weight = jnp.exp2(levels - jnp.max(levels, 0, keepdims=True))
    weight = weight / jnp.sum(weight, 0, keepdims=True)
    weight = jnp.transpose(weight.reshape(NS, HD))
    for i in column:
        for m in range(OWN // PAIR):
            two = pl.ds(m * PAIR, PAIR)
            landed(ro.at[i, two], orecv.at[m, i])
    for n in range(NC):
        for j in range(OWN):
            total = jnp.zeros((ROWS, HD), jnp.float32)
            for i in range(NZ):
                at = i * NC + n
                share = weight[j * ROWS : (j + 1) * ROWS, at : at + 1]
                total = total + share * ro[at, j].astype(jnp.float32)
            for h in range(GROUP):
                at = ((n * OWN + j) * GROUP + h) * HD
                out[:, at : at + HD] = total[h * TOK : (h + 1) * TOK].astype(jnp.bfloat16)
    done = pltpu.make_async_copy(out, o_ref, isem.at[0])
    done.start()
    for copy in sends:
        copy.wait_send()
    done.wait()


def shards(queries, new_keys, new_values, cache_keys, cache_values, start):
    keys = 2 * cache_keys.shape[1] + FRESH
    hbm = pl.BlockSpec(memory_space=pltpu.HBM)
    dma = pltpu.SemaphoreType.DMA
    bf16 = jnp.bfloat16
    f32 = jnp.float32
    return pl.pallas_call(
        kernel,
        out_shape=jax.ShapeDtypeStruct((TOK, HEADS * HD), bf16),
        in_specs=[hbm] * 7,
        out_specs=pl.BlockSpec(memory_space=pl.ANY),
        scratch_shapes=[
            pltpu.SMEM((1,), jnp.int32),
            pltpu.VMEM((1, HD), f32),
            pltpu.VMEM((TOK, HEADS * HD), bf16),
            pltpu.VMEM((TOK, KVH * HD), bf16),
            pltpu.VMEM((TOK, KVH * HD), bf16),
            pltpu.VMEM((KVH, ROWS, HD), bf16),
            pltpu.VMEM((OWN, NS, ROWS, HD), bf16),
            pltpu.VMEM((NY, NC, OWN // PAIR, PAIR, 2 * TOK, HD), bf16),
            pltpu.VMEM((2, KVH, PIECES * PART * TOK, HD), bf16),
            pltpu.VMEM((2, OWN, keys, HD), bf16),
            pltpu.VMEM((OWN, ALL, HD), f32),
            pltpu.VMEM((OWN, ALL, HD), f32),
            pltpu.VMEM((OWN, ALL, HD), f32),
            pltpu.VMEM((NS, OWN, ROWS, HD), bf16),
            pltpu.VMEM((NS, 1, HD), f32),
            pltpu.VMEM((NS, OWN, ROWS, HD), bf16),
            pltpu.VMEM((NS, 1, HD), f32),
            pltpu.VMEM((TOK, HEADS * HD), bf16),
            dma((5,)), dma((6,)), dma((2, NS)), dma((2, NS)), dma((2, NY)), dma((2, NY)),
            dma((2, PIECES, NG)), dma((2, PIECES, NG)), dma((2, NS)), dma((2, NS)), dma((NS,)), dma((NS,)),
        ],
        compiler_params=pltpu.CompilerParams(
            collective_id=0, has_side_effects=True, vmem_limit_bytes=40000 * 1024
        ),
    )(
        start,
        *[
            pltpu.with_memory_space_constraint(one, pltpu.HBM)
            for one in (
                jnp.asarray(frequencies()), queries, new_keys, new_values, cache_keys, cache_values
            )
        ],
    )


def solution(mesh):
    placed = (
        P(("head", "kv"), None),
        P(("head", "kv"), None),
        P(("head", "kv"), None),
        P(None, "kv", None),
        P(None, "kv", None),
        P(),
    )
    return jax.shard_map(
        shards, mesh=mesh, in_specs=placed, out_specs=P(("head", "kv"), None), check_vma=False
    )
```
